512 devices in a mesh: lat: 32 (over x, y), lon: 16 (over z, core).
Axes of the slice: x: 4, y: 8, z: 8, core: 2. Of those that a mesh axis runs over, the one named last changes fastest.
Arguments:
- tracer: float32 [8, 1024, 4096], P(None, 'lat', 'lon'), may hold values from -6 to 6
- thickness: float32 [8, 1024, 4096], P(None, 'lat', 'lon'), may hold values from 0.5 to 2
- land_mask: int32 [8, 1024, 4096], P(None, 'lat', 'lon'), may hold values 0 or 1
- zonal_vel: float32 [8, 1024, 4096], P(None, 'lat', 'lon'), may hold values from -2 to 2
- meridional_vel: float32 [8, 1024, 4096], P(None, 'lat', 'lon'), may hold values from -2 to 2
- surface: float32 [1024, 4096], P('lat', 'lon'), may hold values from -3 to 3
- zonal_baro: float32 [1024, 4096], P('lat', 'lon'), may hold values from -2 to 2
- merid_baro: float32 [1024, 4096], P('lat', 'lon'), may hold values from -2 to 2
Outputs:
- tracer_next: float32 [8, 1024, 4096], P(None, 'lat', 'lon')
- surface_next: float32 [1024, 4096], P('lat', 'lon')
- zonal_next: float32 [1024, 4096], P('lat', 'lon')
- merid_next: float32 [1024, 4096], P('lat', 'lon')
The draws below stay inside these ranges and needn't reach their ends.
All inputs are finite; a program needn't handle non-finite values. No bound on the sum of `land_mask` on one device may be relied on, other than what follows from the above.
Results may differ from the reference program's by a relative error of at most 0.00002.
Values sent between devices are 32-bit elements; how exact they have to be, the bound alone decides.
A program may use at most 64 MiB of HBM per device.

```python
import math
import jax
import jax.numpy as jnp

K = 8
SUB = 8
NLAT = 1024
NLON = 4096


def plant(result, key, low, top_value):
    place = [jax.random.randint(jax.random.fold_in(key, axis), (), 0, length) for axis, length in enumerate(result.shape)]
    main_axis = result.shape.index(max(result.shape))
    neighbour = place[:main_axis] + [(place[main_axis] + 1) % result.shape[main_axis]] + place[main_axis + 1:]
    return result.at[tuple(place)].set(low).at[tuple(neighbour)].set(top_value)


def shard_levels(stream_key, dims, split, least, top_value):
    def one(position, shards_of):
        heights = jax.random.uniform(jax.random.fold_in(jax.random.fold_in(stream_key, 6), position), (shards_of,), jnp.float32, least / len(split), top_value / len(split))
        return jnp.repeat(jnp.exp(heights), dims[position] // shards_of).reshape((-1,) + (1,) * (len(dims) - position - 1))

    gain = one(*split[0])
    for cut in split[1:]:
        gain = gain * one(*cut)
    return gain


def gaussian(stream_key, dims, spread, reach, split=(), held_as=jnp.bfloat16):
    entries = spread * jax.random.normal(stream_key, dims, jnp.float32)
    if split:
        entries = entries * shard_levels(stream_key, dims, split, -0.22, 0.18)
    return jnp.clip(entries, -reach, reach).astype(held_as)


def setup_inputs(seed: int = 0) -> dict:
    seeds = jax.random.split(jax.random.key(seed), 9)
    return {
        "tracer": gaussian(seeds[0], (K, NLAT, NLON), 1.0, 6.0, ((1, 32), (2, 16)), jnp.float32),
        "thickness": jnp.clip(jnp.exp(math.log(2.0) - 1.3862944 * jax.random.uniform(seeds[1], (K, NLAT, NLON), jnp.float32) ** shard_levels(seeds[1], (K, NLAT, NLON), ((1, 32), (2, 16)), -0.2, 0.2)), 0.5, 2.0),
        "land_mask": plant((jax.random.randint(seeds[2], (K, NLAT, NLON), 0, 10) < 7).astype(jnp.int32), jax.random.fold_in(seeds[2], 1), 0, 1),
        "zonal_vel": gaussian(seeds[3], (K, NLAT, NLON), 0.3, 2.0, ((1, 32), (2, 16)), jnp.float32),
        "meridional_vel": gaussian(seeds[4], (K, NLAT, NLON), 0.3, 2.0, ((1, 32), (2, 16)), jnp.float32),
        "surface": gaussian(seeds[5], (NLAT, NLON), 0.5, 3.0, ((0, 32), (1, 16)), jnp.float32),
        "zonal_baro": gaussian(seeds[6], (NLAT, NLON), 0.3, 2.0, ((0, 32), (1, 16)), jnp.float32),
        "merid_baro": gaussian(seeds[7], (NLAT, NLON), 0.3, 2.0, ((0, 32), (1, 16)), jnp.float32),
    }


def pad_rows(field, width, sign):
    wrapped = jnp.concatenate([field[..., -width:], field, field[..., :width]], axis=-1)
    upper = sign * jnp.flip(wrapped[..., -width:, :], (-2, -1))
    lower = jnp.zeros_like(upper)
    return jnp.concatenate([lower, wrapped, upper], axis=-2)


def tracer_update(padded_t, padded_h, padded_u, padded_v, wet_cells, thickness):
    center_t = padded_t[:, 1:-1, 1:-1]
    center_h = padded_h[:, 1:-1, 1:-1]
    east_depth = jnp.minimum(padded_h[:, 1:-1, :-1], padded_h[:, 1:-1, 1:])
    east_flux = east_depth * (0.25 * (padded_u[:, 1:-1, :-1] + padded_u[:, 1:-1, 1:]) * (padded_t[:, 1:-1, :-1] + padded_t[:, 1:-1, 1:]) - 0.1 * (padded_t[:, 1:-1, 1:] - padded_t[:, 1:-1, :-1]))
    north_depth = jnp.minimum(padded_h[:, :-1, 1:-1], padded_h[:, 1:, 1:-1])
    north_flux = north_depth * (0.25 * (padded_v[:, :-1, 1:-1] + padded_v[:, 1:, 1:-1]) * (padded_t[:, :-1, 1:-1] + padded_t[:, 1:, 1:-1]) - 0.1 * (padded_t[:, 1:, 1:-1] - padded_t[:, :-1, 1:-1]))
    vertical = 0.2 * jnp.minimum(center_h[:-1], center_h[1:]) * (center_t[1:] - center_t[:-1])
    zero_level = jnp.zeros_like(center_t[:1])
    vertical_div = jnp.concatenate([vertical, zero_level], axis=0) - jnp.concatenate([zero_level, vertical], axis=0)
    tendency = vertical_div - (east_flux[:, :, 1:] - east_flux[:, :, :-1]) - (north_flux[:, 1:, :] - north_flux[:, :-1, :])
    return center_t + 0.2 * wet_cells / thickness * tendency


def subcycle(height, zonal, merid, depth, force_u, force_v):
    wet = jnp.minimum(2.0 * depth, 1.0)
    east_flux = jnp.minimum(depth[:, :-1], depth[:, 1:]) * 0.5 * (zonal[:, :-1] + zonal[:, 1:])
    north_flux = jnp.minimum(depth[:-1], depth[1:]) * 0.5 * (merid[:-1] + merid[1:])
    divergence = east_flux[1:-1, 1:] - east_flux[1:-1, :-1] + north_flux[1:, 1:-1] - north_flux[:-1, 1:-1]
    height_new = height[1:-1, 1:-1] - 0.2 * wet[1:-1, 1:-1] * divergence
    slope_x = 0.5 * (height_new[1:-1, 2:] - height_new[1:-1, :-2])
    slope_y = 0.5 * (height_new[2:, 1:-1] - height_new[:-2, 1:-1])
    inner = wet[2:-2, 2:-2]
    zonal_new = inner * (zonal[2:-2, 2:-2] - 0.2 * 0.5 * slope_x + 0.2 * force_u[2:-2, 2:-2])
    merid_new = inner * (merid[2:-2, 2:-2] - 0.2 * 0.5 * slope_y + 0.2 * force_v[2:-2, 2:-2])
    return height_new[1:-1, 1:-1], zonal_new, merid_new


def reference(tracer, thickness, land_mask, zonal_vel, meridional_vel, surface, zonal_baro, merid_baro):
    wet_cells = land_mask.astype(jnp.float32)
    wet_thick = wet_cells * thickness
    depth = jnp.sum(wet_thick, axis=0)
    force_u = 0.05 * jnp.sum(wet_thick * zonal_vel, axis=0)
    force_v = 0.05 * jnp.sum(wet_thick * meridional_vel, axis=0)
    tracer_next = tracer_update(pad_rows(tracer, 1, 1.0), pad_rows(wet_thick, 1, 1.0), pad_rows(zonal_vel, 1, -1.0), pad_rows(meridional_vel, 1, -1.0), wet_cells, thickness)
    depth_pad = pad_rows(depth, 2, 1.0)
    force_u_pad = pad_rows(force_u, 2, -1.0)
    force_v_pad = pad_rows(force_v, 2, -1.0)
    height, zonal, merid = surface, zonal_baro, merid_baro
    for number in range(SUB):
        height, zonal, merid = subcycle(pad_rows(height, 2, 1.0), pad_rows(zonal, 2, -1.0), pad_rows(merid, 2, -1.0), depth_pad, force_u_pad, force_v_pad)
    return tracer_next, height, zonal, merid
```

```python
import functools

import jax
import jax.numpy as jnp
from jax import lax
from jax.experimental import pallas as pl
from jax.experimental.pallas import tpu as pltpu
from jax.sharding import PartitionSpec as P

SUB = 8
HALO = 2 * SUB
MESH = pl.DeviceIdType.MESH

ST_N, ST_S, CF_N, CF_S = 0, 3, 6, 7
P_E, P_W, P_NE, P_SE, P_NW, P_SW = 8, 9, 10, 11, 12, 13
T_N, T_S, T_E, T_W = 14, 15, 16, 17
SLOTS = 18
UP_ST, DN_ST, UP_CF, DN_CF = 0, 3, 6, 7
SD_E, SD_W, SD_EU, SD_ED, SD_WU, SD_WD = 8, 9, 10, 11, 12, 13
SD_TU, SD_TD, SD_TE, SD_TW = 14, 15, 16, 17


def lanes(shape):
    return lax.broadcasted_iota(jnp.int32, shape, 1)


def flip_rows(tile):
    rows = tile.shape[0]
    index = 7 - lax.broadcasted_iota(jnp.int32, (8, 128), 0)
    parts = [
        jnp.take_along_axis(tile[r : r + 8], index, axis=0) for r in range(rows - 8, -8, -8)
    ]
    return jnp.concatenate(parts, axis=0)


def flip_lanes(tile, mask):
    index = lanes((8, 128)) ^ mask
    parts = [
        jnp.take_along_axis(tile[r : r + 8], index, axis=1) for r in range(0, tile.shape[0], 8)
    ]
    return jnp.concatenate(parts, axis=0)


def kernel(
    n_lat, n_lon,
    tr, th, mk, zu, mv, sf, zb, mb,
    o_tr, o_sf, o_zb, o_mb,
    t_v, h_v, m_v, u_v, v_v, w_v, c_v, out_v,
    x_v, y_v, a_v, pe, pw, re, rw, qe, qw, se, sw, gn, gs, hn, hs,
    load_sem, out_sem, send_sem, recv_sem,
):
    levels, rows, columns = t_v.shape
    wide = columns + 128
    top = HALO + rows
    lat, lon = lax.axis_index("lat"), lax.axis_index("lon")
    last, first = lat == n_lat - 1, lat == 0
    not_last, not_first = lat < n_lat - 1, lat > 0
    east, west = lax.rem(lon + 1, n_lon), lax.rem(lon + n_lon - 1, n_lon)
    mirror = n_lon - 1 - lon
    fold_e = lax.rem(2 * n_lon - 2 - lon, n_lon)
    fold_w = lax.rem(n_lon - lon, n_lon)
    self_e, self_w = fold_e == lon, fold_w == lon

    loads = [
        (th, h_v), (mk, m_v), (zu, u_v), (mv, v_v), (tr, t_v),
        (sf, x_v.at[0, pl.ds(HALO, rows), pl.ds(0, columns)]),
        (zb, x_v.at[1, pl.ds(HALO, rows), pl.ds(0, columns)]),
        (mb, x_v.at[2, pl.ds(HALO, rows), pl.ds(0, columns)]),
    ]
    loads = [pltpu.make_async_copy(s, d, load_sem.at[i]) for i, (s, d) in enumerate(loads)]
    for load in loads:
        load.start()

    barrier = pltpu.get_barrier_semaphore()

    def greet(to_lat, to_lon):
        pl.semaphore_signal(barrier, inc=1, device_id=(to_lat, to_lon), device_id_type=MESH)

    greet(lat, east)
    greet(lat, west)

    @pl.when(not_last)
    def _():
        greet(lat + 1, lon)
        greet(lat + 1, east)
        greet(lat + 1, west)

    @pl.when(not_first)
    def _():
        greet(lat - 1, lon)
        greet(lat - 1, east)
        greet(lat - 1, west)

    @pl.when(last)
    def _():
        greet(lat, mirror)

    @pl.when(last & jnp.logical_not(self_e))
    def _():
        greet(lat, fold_e)

    @pl.when(last & jnp.logical_not(self_w))
    def _():
        greet(lat, fold_w)

    def send(src, dst, out_slot, in_slot, to_lat, to_lon):
        return pltpu.make_async_remote_copy(
            src_ref=src, dst_ref=dst, send_sem=send_sem.at[out_slot],
            recv_sem=recv_sem.at[in_slot], device_id=(to_lat, to_lon), device_id_type=MESH,
        )

    def arrived(dst, in_slot):
        send(dst, dst, 0, in_slot, lat, east).wait_recv()

    def sent(src, out_slot):
        send(src, src, out_slot, 0, lat, east).wait_send()

    low, high = pl.ds(0, HALO), pl.ds(top, HALO)
    own_low, own_high = pl.ds(HALO, HALO), pl.ds(rows, HALO)
    all_columns = pl.ds(0, columns)
    state = (sf, zb, mb)

    def barrier_wait():
        ups = jnp.where(
            last, 1 + jnp.where(self_e, 0, 1) + jnp.where(self_w, 0, 1), 3
        )
        pl.semaphore_wait(barrier, 2 + ups + jnp.where(first, 0, 3))

    def send_state():
        for f in range(3):
            src = state[f].at[pl.ds(rows - HALO, HALO), :]

            @pl.when(not_last)
            def _():
                send(src, x_v.at[f, low, all_columns], UP_ST + f, ST_S + f, lat + 1, lon).start()

            @pl.when(last)
            def _():
                send(src, x_v.at[f, high, all_columns], UP_ST + f, ST_N + f, lat, mirror).start()

            @pl.when(not_first)
            def _():
                send(
                    state[f].at[low, :], x_v.at[f, high, all_columns],
                    DN_ST + f, ST_N + f, lat - 1, lon,
                ).start()

    def send_column():
        src = y_v.at[:, own_high, all_columns]

        @pl.when(not_last)
        def _():
            send(src, y_v.at[:, low, all_columns], UP_CF, CF_S, lat + 1, lon).start()

        @pl.when(last)
        def _():
            send(src, y_v.at[:, high, all_columns], UP_CF, CF_N, lat, mirror).start()

        @pl.when(not_first)
        def _():
            send(
                y_v.at[:, own_low, all_columns], y_v.at[:, high, all_columns],
                DN_CF, CF_N, lat - 1, lon,
            ).start()

    part_low, part_high = pl.ds(0, HALO), pl.ds(rows - HALO, HALO)
    middle = pl.ds(HALO, rows)

    def send_sides():
        send(pe, rw.at[middle], SD_E, P_W, lat, east).start()
        send(pw, re.at[middle], SD_W, P_E, lat, west).start()

        @pl.when(not_last)
        def _():
            send(pe.at[part_high], rw.at[low], SD_EU, P_SW, lat + 1, east).start()
            send(pw.at[part_high], re.at[low], SD_WU, P_SE, lat + 1, west).start()

        @pl.when(last & jnp.logical_not(self_e))
        def _():
            send(pe.at[part_high], re.at[high], SD_EU, P_NE, lat, fold_e).start()

        @pl.when(last & self_e)
        def _():
            pltpu.make_async_copy(pe.at[part_high], re.at[high], recv_sem.at[P_NE]).start()

        @pl.when(last & jnp.logical_not(self_w))
        def _():
            send(pw.at[part_high], rw.at[high], SD_WU, P_NW, lat, fold_w).start()

        @pl.when(last & self_w)
        def _():
            pltpu.make_async_copy(pw.at[part_high], rw.at[high], recv_sem.at[P_NW]).start()

        @pl.when(not_first)
        def _():
            send(pe.at[part_low], rw.at[high], SD_ED, P_NW, lat - 1, east).start()
            send(pw.at[part_low], re.at[high], SD_WD, P_NE, lat - 1, west).start()

    def send_tracer():
        @pl.when(not_last)
        def _():
            send(gn, hs, SD_TU, T_S, lat + 1, lon).start()

        @pl.when(last)
        def _():
            send(gn, hn, SD_TU, T_N, lat, mirror).start()

        @pl.when(not_first)
        def _():
            send(gs, hn, SD_TD, T_N, lat - 1, lon).start()

        send(qe, sw, SD_TE, T_W, lat, east).start()
        send(qw, se, SD_TW, T_E, lat, west).start()

    barrier_wait()
    send_state()

    for load in loads[:4]:
        load.wait()

    def add_level(k, sums):
        wet = m_v[k].astype(jnp.float32) * h_v[k]
        w_v[k] = wet
        return sums[0] + wet, sums[1] + wet * u_v[k], sums[2] + wet * v_v[k]

    zero = jnp.zeros((rows, columns), jnp.float32)
    depth, force_u, force_v = lax.fori_loop(0, levels, add_level, (zero, zero, zero))
    force_u, force_v = 0.05 * force_u, 0.05 * force_v
    y_v[0, pl.ds(HALO, rows), all_columns] = depth
    y_v[1, pl.ds(HALO, rows), all_columns] = force_u
    y_v[2, pl.ds(HALO, rows), all_columns] = force_v
    send_column()

    for load in loads[4:]:
        load.wait()

    lane = lanes((rows, 128))
    fields = [x_v[f, pl.ds(HALO, rows), all_columns] for f in range(3)] + [depth, force_u, force_v]
    pack_e = jnp.zeros((rows, 128), jnp.float32)
    pack_w = jnp.zeros((rows, 128), jnp.float32)
    for f in range(6):
        here = (lane >= HALO * f) & (lane < HALO * (f + 1))
        from_e = pltpu.roll(fields[f][:, columns - 128 :], (HALO * f + HALO) % 128, 1)
        pack_e = jnp.where(here, from_e, pack_e)
        from_w = fields[f][:, :128]
        if f:
            from_w = pltpu.roll(from_w, HALO * f, 1)
        pack_w = jnp.where(here, from_w, pack_w)
    pe[...] = pack_e
    pw[...] = pack_w
    send_sides()

    pack_e = jnp.zeros((rows, 128), jnp.float32)
    pack_w = jnp.zeros((rows, 128), jnp.float32)
    for i, source in enumerate((t_v, w_v, u_v)):
        for k in range(levels):
            slot = i * levels + k
            pack_e = jnp.where(
                lane == slot, pltpu.roll(source[k, :, columns - 128 :], slot + 1, 1), pack_e
            )
            from_w = source[k, :, :128]
            if slot:
                from_w = pltpu.roll(from_w, slot, 1)
            pack_w = jnp.where(lane == slot, from_w, pack_w)
    qe[...] = pack_e
    qw[...] = pack_w
    for i, source in enumerate((t_v, w_v, v_v)):
        gn[i] = source[:, rows - 1, :]
        gs[i] = source[:, 0, :]
    send_tracer()

    col = lanes((rows, columns))
    row = lax.broadcasted_iota(jnp.int32, (rows, columns), 0)

    def tracer_level(k, lower):
        t, w, u, v = t_v[k], w_v[k], u_v[k], v_v[k]
        t_e, w_e, u_e = (pltpu.roll(z, columns - 1, 1) for z in (t, w, u))
        flux = jnp.minimum(w, w_e) * (0.25 * (u + u_e) * (t + t_e) - 0.1 * (t_e - t))
        flux = jnp.where(col == columns - 1, 0.0, flux)
        flow = flux - pltpu.roll(flux, 1, 1)
        t_n, w_n, v_n = (pltpu.roll(z, rows - 1, 0) for z in (t, w, v))
        flux = jnp.minimum(w, w_n) * (0.25 * (v + v_n) * (t + t_n) - 0.1 * (t_n - t))
        flux = jnp.where(row == rows - 1, 0.0, flux)
        flow = flow + (flux - pltpu.roll(flux, 1, 0))
        above = jnp.minimum(k + 1, levels - 1)
        upper = 0.2 * jnp.minimum(w, w_v[above]) * (t_v[above] - t)
        scale = 0.2 * m_v[k].astype(jnp.float32) / h_v[k]
        c_v[k] = scale
        out_v[k] = t + scale * ((upper - lower) - flow)
        return upper

    lax.fori_loop(0, levels, tracer_level, zero)

    for f in range(3):
        arrived(x_v.at[f, high, all_columns], ST_N + f)
    arrived(y_v.at[:, high, all_columns], CF_N)
    arrived(re.at[middle], P_E)
    arrived(rw.at[middle], P_W)
    arrived(re.at[high], P_NE)
    arrived(rw.at[high], P_NW)

    @pl.when(not_first)
    def _():
        for f in range(3):
            arrived(x_v.at[f, low, all_columns], ST_S + f)
        arrived(y_v.at[:, low, all_columns], CF_S)
        arrived(re.at[low], P_SE)
        arrived(rw.at[low], P_SW)

    @pl.when(first)
    def _():
        for ref in (x_v, y_v):
            for f in range(3):
                ref[f, low, all_columns] = jnp.zeros((HALO, columns), jnp.float32)
        re[low] = jnp.zeros((HALO, 128), jnp.float32)
        rw[low] = jnp.zeros((HALO, 128), jnp.float32)

    @pl.when(last)
    def _():
        for ref in (x_v, y_v):
            for f in range(3):
                sign = 1.0 if f == 0 else -1.0
                old = ref[f, high, all_columns]
                tiles = [old[:, c : c + 128] for c in range(columns - 128, -128, -128)]
                new = jnp.concatenate([flip_lanes(flip_rows(t), 127) for t in tiles], axis=1)
                ref[f, high, all_columns] = sign * new
        field = lanes((HALO, 128)) // HALO
        even = (field == 0) | (field == 3)
        for ref in (re, rw):
            new = flip_lanes(flip_rows(ref[high]), HALO - 1)
            ref[high] = jnp.where(even, new, -new)

    ext = x_v.shape[1]
    lane = lanes((ext, 128))
    from_e, from_w = re[...], rw[...]
    for f in range(6):
        shift = (128 - HALO * f) % 128
        tile_e = pltpu.roll(from_e, shift, 1) if shift else from_e
        shift = 128 - HALO - HALO * f
        tile_w = pltpu.roll(from_w, shift, 1) if shift else from_w
        ref = x_v if f < 3 else y_v
        ref[f % 3, :, pl.ds(columns, 128)] = jnp.where(lane < 64, tile_e, tile_w)

    d = y_v[0]
    a_v[0] = jnp.minimum(2.0 * d, 1.0)
    a_v[1] = 0.5 * jnp.minimum(d, pltpu.roll(d, wide - 1, 1))
    a_v[2] = 0.5 * jnp.minimum(d, pltpu.roll(d, ext - 1, 0))
    a_v[3] = 0.2 * y_v[1]
    a_v[4] = 0.2 * y_v[2]

    def cycles(span):
        count = span.size

        def step(_, carry):
            eta, ub, vb = (x_v[f, span, :] for f in range(3))
            wet = a_v[0, span, :]
            flux = a_v[1, span, :] * (ub + pltpu.roll(ub, wide - 1, 1))
            div = flux - pltpu.roll(flux, 1, 1)
            flux = a_v[2, span, :] * (vb + pltpu.roll(vb, count - 1, 0))
            div = div + (flux - pltpu.roll(flux, 1, 0))
            eta = eta - 0.2 * wet * div
            slope_x = pltpu.roll(eta, wide - 1, 1) - pltpu.roll(eta, 1, 1)
            slope_y = pltpu.roll(eta, count - 1, 0) - pltpu.roll(eta, 1, 0)
            x_v[0, span, :] = eta
            x_v[1, span, :] = wet * (ub - 0.05 * slope_x + a_v[3, span, :])
            x_v[2, span, :] = wet * (vb - 0.05 * slope_y + a_v[4, span, :])
            return carry

        lax.fori_loop(0, SUB // 2, step, 0)

    cycles(pl.ds(0, ext))
    cycles(pl.ds(SUB, ext - HALO))

    outs = [
        pltpu.make_async_copy(
            x_v.at[f, pl.ds(HALO, rows), all_columns], (o_sf, o_zb, o_mb)[f], out_sem.at[f]
        )
        for f in range(3)
    ]
    for out in outs:
        out.start()

    arrived(hn, T_N)
    arrived(se, T_E)
    arrived(sw, T_W)

    @pl.when(not_first)
    def _():
        arrived(hs, T_S)

    @pl.when(first)
    def _():
        hs[...] = jnp.zeros(hs.shape, jnp.float32)

    @pl.when(last)
    def _():
        for i in range(3):
            sign = -1.0 if i == 2 else 1.0
            old = hn[i]
            tiles = [old[:, c : c + 128] for c in range(columns - 128, -128, -128)]
            hn[i] = sign * jnp.concatenate([flip_lanes(t, 127) for t in tiles], axis=1)

    def face(t_a, t_b, w_a, w_b, u_a, u_b):
        return jnp.minimum(w_a, w_b) * (0.25 * (u_a + u_b) * (t_a + t_b) - 0.1 * (t_b - t_a))

    def packed_face(a, b):
        a_1, b_1 = pltpu.roll(a, 128 - levels, 1), pltpu.roll(b, 128 - levels, 1)
        a_2, b_2 = pltpu.roll(a, 128 - 2 * levels, 1), pltpu.roll(b, 128 - 2 * levels, 1)
        return face(a, b, a_1, b_1, a_2, b_2)

    flux_e = packed_face(qe[...], se[...])
    flux_w = packed_face(sw[...], qw[...])
    lane = lanes((rows, 128))
    for k in range(levels):
        edge = pl.ds(columns - 128, 128)
        moved = pltpu.roll(flux_e, 127 - k, 1)
        out_v[k, :, edge] = out_v[k, :, edge] - jnp.where(
            lane == 127, c_v[k, :, edge] * moved, 0.0
        )
        edge = pl.ds(0, 128)
        moved = pltpu.roll(flux_w, 128 - k, 1) if k else flux_w
        out_v[k, :, edge] = out_v[k, :, edge] + jnp.where(lane == 0, c_v[k, :, edge] * moved, 0.0)
    flux_n = face(gn[0], hn[0], gn[1], hn[1], gn[2], hn[2])
    out_v[:, rows - 1, :] = out_v[:, rows - 1, :] - c_v[:, rows - 1, :] * flux_n
    flux_s = face(hs[0], gs[0], hs[1], gs[1], hs[2], gs[2])
    out_v[:, 0, :] = out_v[:, 0, :] + c_v[:, 0, :] * flux_s

    out = pltpu.make_async_copy(out_v, o_tr, out_sem.at[3])
    out.start()

    for f in range(3):
        sent(state[f].at[low, :], UP_ST + f)
    sent(y_v.at[:, low, all_columns], UP_CF)
    sent(pe, SD_E)
    sent(pw, SD_W)
    sent(gn, SD_TU)
    sent(qe, SD_TE)
    sent(qw, SD_TW)

    @pl.when(not_last | jnp.logical_not(self_e))
    def _():
        sent(pe.at[part_high], SD_EU)

    @pl.when(not_last | jnp.logical_not(self_w))
    def _():
        sent(pw.at[part_high], SD_WU)

    @pl.when(not_first)
    def _():
        for f in range(3):
            sent(state[f].at[low, :], DN_ST + f)
        sent(y_v.at[:, low, all_columns], DN_CF)
        sent(pe.at[part_low], SD_ED)
        sent(pw.at[part_low], SD_WD)
        sent(gs, SD_TD)

    for copy in outs:
        copy.wait()
    out.wait()


def on_device(n_lat, n_lon, *args):
    levels, rows, columns = args[0].shape
    block = pltpu.VMEM((levels, rows, columns), jnp.float32)
    ext, wide = rows + 2 * HALO, columns + 128
    strip, long_strip = pltpu.VMEM((rows, 128), jnp.float32), pltpu.VMEM((ext, 128), jnp.float32)
    line = pltpu.VMEM((3, levels, columns), jnp.float32)
    flat = pltpu.VMEM((3, ext, wide), jnp.float32)
    scratch = [block, block, pltpu.VMEM((levels, rows, columns), jnp.int32)] + [block] * 5
    scratch += [flat] * 2 + [pltpu.VMEM((5, ext, wide), jnp.float32)] + [strip] * 2 + [long_strip] * 2 + [strip] * 4 + [line] * 4
    scratch += [
        pltpu.SemaphoreType.DMA((8,)), pltpu.SemaphoreType.DMA((4,)),
        pltpu.SemaphoreType.DMA((SLOTS,)), pltpu.SemaphoreType.DMA((SLOTS,)),
    ]
    whole = jax.ShapeDtypeStruct((levels, rows, columns), jnp.float32)
    surface = jax.ShapeDtypeStruct((rows, columns), jnp.float32)
    return pl.pallas_call(
        functools.partial(kernel, n_lat, n_lon),
        out_shape=(whole, surface, surface, surface),
        in_specs=[pl.BlockSpec(memory_space=pl.ANY)] * 8,
        out_specs=(pl.BlockSpec(memory_space=pl.ANY),) * 4,
        scratch_shapes=scratch,
        compiler_params=pltpu.CompilerParams(collective_id=0, has_side_effects=True),
        name="ocean",
    )(*args)


def solution(mesh):
    whole, surface = P(None, "lat", "lon"), P("lat", "lon")
    return jax.shard_map(
        functools.partial(on_device, mesh.shape["lat"], mesh.shape["lon"]),
        mesh=mesh,
        in_specs=(whole,) * 5 + (surface,) * 3,
        out_specs=(whole, surface, surface, surface),
        check_vma=False,
    )
```

```python
import functools

import jax
import jax.numpy as jnp
from jax import lax
from jax.experimental import pallas as pl
from jax.experimental.pallas import tpu as pltpu
from jax.sharding import PartitionSpec as P

SUB = 8
HALO = 2 * SUB
MESH = pl.DeviceIdType.MESH

F_N, F_S, P_E, P_W, P_NE, P_SE, P_NW, P_SW, T_N, T_S, T_E, T_W = range(12)
UP_F, DN_F, SD_E, SD_W, SD_EU, SD_ED, SD_WU, SD_WD, SD_TU, SD_TD, SD_TE, SD_TW = range(12)
SLOTS = 12


def lanes(shape):
    return lax.broadcasted_iota(jnp.int32, shape, 1)


def flip_rows(tile):
    rows = tile.shape[0]
    index = 7 - lax.broadcasted_iota(jnp.int32, (8, 128), 0)
    parts = [
        jnp.take_along_axis(tile[r : r + 8], index, axis=0) for r in range(rows - 8, -8, -8)
    ]
    return jnp.concatenate(parts, axis=0)


def flip_lanes(tile, mask):
    index = lanes((8, 128)) ^ mask
    parts = [
        jnp.take_along_axis(tile[r : r + 8], index, axis=1) for r in range(0, tile.shape[0], 8)
    ]
    return jnp.concatenate(parts, axis=0)


def kernel(
    n_lat, n_lon,
    tr, th, mk, zu, mv, sf, zb, mb,
    out_v, o_st,
    t_v, h_v, m_v, u_v, v_v, w_v, c_v,
    f_v, a_v, pe, pw, re, rw, qe, qw, se, sw, gn, gs, hn, hs,
    load_sem, send_sem, recv_sem,
):
    levels, rows, columns = t_v.shape
    wide = columns + 128
    top = HALO + rows
    lat, lon = lax.axis_index("lat"), lax.axis_index("lon")
    last, first = lat == n_lat - 1, lat == 0
    not_last, not_first = lat < n_lat - 1, lat > 0
    east, west = lax.rem(lon + 1, n_lon), lax.rem(lon + n_lon - 1, n_lon)
    mirror = n_lon - 1 - lon
    fold_e = lax.rem(2 * n_lon - 2 - lon, n_lon)
    fold_w = lax.rem(n_lon - lon, n_lon)
    self_e, self_w = fold_e == lon, fold_w == lon

    low, middle, high = pl.ds(0, HALO), pl.ds(HALO, rows), pl.ds(top, HALO)
    own_low, own_high = pl.ds(HALO, HALO), pl.ds(rows, HALO)
    part_low, part_high = pl.ds(0, HALO), pl.ds(rows - HALO, HALO)
    all_columns = pl.ds(0, columns)

    loads = [
        (th, h_v), (mk, m_v), (zu, u_v), (mv, v_v), (tr, t_v),
        (sf, f_v.at[0, middle, all_columns]),
        (zb, f_v.at[1, middle, all_columns]),
        (mb, f_v.at[2, middle, all_columns]),
    ]
    loads = [pltpu.make_async_copy(s, d, load_sem.at[i]) for i, (s, d) in enumerate(loads)]

    barrier = pltpu.get_barrier_semaphore()

    def greet(to_lat, to_lon):
        pl.semaphore_signal(barrier, inc=1, device_id=(to_lat, to_lon), device_id_type=MESH)

    greet(lat, east)
    greet(lat, west)

    @pl.when(not_last)
    def _():
        greet(lat + 1, lon)
        greet(lat + 1, east)
        greet(lat + 1, west)

    @pl.when(not_first)
    def _():
        greet(lat - 1, lon)
        greet(lat - 1, east)
        greet(lat - 1, west)

    @pl.when(last)
    def _():
        greet(lat, mirror)

    @pl.when(last & jnp.logical_not(self_e))
    def _():
        greet(lat, fold_e)

    @pl.when(last & jnp.logical_not(self_w))
    def _():
        greet(lat, fold_w)

    for load in loads:
        load.start()

    def send(src, dst, out_slot, in_slot, to_lat, to_lon):
        return pltpu.make_async_remote_copy(
            src_ref=src, dst_ref=dst, send_sem=send_sem.at[out_slot],
            recv_sem=recv_sem.at[in_slot], device_id=(to_lat, to_lon), device_id_type=MESH,
        )

    def arrived(dst, in_slot):
        send(dst, dst, 0, in_slot, lat, east).wait_recv()

    def sent(src, out_slot):
        send(src, src, out_slot, 0, lat, east).wait_send()


    def barrier_wait():
        ups = jnp.where(
            last, 1 + jnp.where(self_e, 0, 1) + jnp.where(self_w, 0, 1), 3
        )
        pl.semaphore_wait(barrier, 2 + ups + jnp.where(first, 0, 3))

    def send_fields():
        src = f_v.at[:, own_high, all_columns]

        @pl.when(not_last)
        def _():
            send(src, f_v.at[:, low, all_columns], UP_F, F_S, lat + 1, lon).start()

        @pl.when(last)
        def _():
            send(src, f_v.at[:, high, all_columns], UP_F, F_N, lat, mirror).start()

        @pl.when(not_first)
        def _():
            send(
                f_v.at[:, own_low, all_columns], f_v.at[:, high, all_columns],
                DN_F, F_N, lat - 1, lon,
            ).start()

    def send_sides():
        send(pe, rw.at[middle], SD_E, P_W, lat, east).start()
        send(pw, re.at[middle], SD_W, P_E, lat, west).start()

        @pl.when(not_last)
        def _():
            send(pe.at[part_high], rw.at[low], SD_EU, P_SW, lat + 1, east).start()
            send(pw.at[part_high], re.at[low], SD_WU, P_SE, lat + 1, west).start()

        @pl.when(last & jnp.logical_not(self_e))
        def _():
            send(pe.at[part_high], re.at[high], SD_EU, P_NE, lat, fold_e).start()

        @pl.when(last & self_e)
        def _():
            pltpu.make_async_copy(pe.at[part_high], re.at[high], recv_sem.at[P_NE]).start()

        @pl.when(last & jnp.logical_not(self_w))
        def _():
            send(pw.at[part_high], rw.at[high], SD_WU, P_NW, lat, fold_w).start()

        @pl.when(last & self_w)
        def _():
            pltpu.make_async_copy(pw.at[part_high], rw.at[high], recv_sem.at[P_NW]).start()

        @pl.when(not_first)
        def _():
            send(pe.at[part_low], rw.at[high], SD_ED, P_NW, lat - 1, east).start()
            send(pw.at[part_low], re.at[high], SD_WD, P_NE, lat - 1, west).start()

    def send_tracer():
        @pl.when(not_last)
        def _():
            send(gn, hs, SD_TU, T_S, lat + 1, lon).start()

        @pl.when(last)
        def _():
            send(gn, hn, SD_TU, T_N, lat, mirror).start()

        @pl.when(not_first)
        def _():
            send(gs, hn, SD_TD, T_N, lat - 1, lon).start()

        send(qe, sw, SD_TE, T_W, lat, east).start()
        send(qw, se, SD_TW, T_E, lat, west).start()

    for load in loads[:4]:
        load.wait()

    def add_level(k, sums):
        wet = m_v[k].astype(jnp.float32) * h_v[k]
        w_v[k] = wet
        return sums[0] + wet, sums[1] + wet * u_v[k], sums[2] + wet * v_v[k]

    zero = jnp.zeros((rows, columns), jnp.float32)
    depth, force_u, force_v = lax.fori_loop(0, levels, add_level, (zero, zero, zero))
    force_u, force_v = 0.05 * force_u, 0.05 * force_v
    f_v[3, middle, all_columns] = depth
    f_v[4, middle, all_columns] = force_u
    f_v[5, middle, all_columns] = force_v

    for load in loads[4:]:
        load.wait()

    lane = lanes((rows, 128))
    fields = [f_v[f, middle, all_columns] for f in range(3)] + [depth, force_u, force_v]
    pack_e = jnp.zeros((rows, 128), jnp.float32)
    pack_w = jnp.zeros((rows, 128), jnp.float32)
    for f in range(6):
        here = (lane >= HALO * f) & (lane < HALO * (f + 1))
        from_e = pltpu.roll(fields[f][:, columns - 128 :], (HALO * f + HALO) % 128, 1)
        pack_e = jnp.where(here, from_e, pack_e)
        from_w = fields[f][:, :128]
        if f:
            from_w = pltpu.roll(from_w, HALO * f, 1)
        pack_w = jnp.where(here, from_w, pack_w)
    pe[...] = pack_e
    pw[...] = pack_w
    barrier_wait()
    send_sides()
    send_fields()

    pack_e = jnp.zeros((rows, 128), jnp.float32)
    pack_w = jnp.zeros((rows, 128), jnp.float32)
    for i, source in enumerate((t_v, w_v, u_v)):
        for k in range(levels):
            slot = i * levels + k
            pack_e = jnp.where(
                lane == slot, pltpu.roll(source[k, :, columns - 128 :], slot + 1, 1), pack_e
            )
            from_w = source[k, :, :128]
            if slot:
                from_w = pltpu.roll(from_w, slot, 1)
            pack_w = jnp.where(lane == slot, from_w, pack_w)
    qe[...] = pack_e
    qw[...] = pack_w
    for i, source in enumerate((t_v, w_v, v_v)):
        gn[i] = source[:, rows - 1, :]
        gs[i] = source[:, 0, :]
    send_tracer()

    col = lanes((rows, columns))
    row = lax.broadcasted_iota(jnp.int32, (rows, columns), 0)

    def tracer_level(k, lower):
        t, w, u, v = t_v[k], w_v[k], u_v[k], v_v[k]
        t_e, w_e, u_e = (pltpu.roll(z, columns - 1, 1) for z in (t, w, u))
        flux = jnp.minimum(w, w_e) * (0.25 * (u + u_e) * (t + t_e) - 0.1 * (t_e - t))
        flux = jnp.where(col == columns - 1, 0.0, flux)
        flow = flux - pltpu.roll(flux, 1, 1)
        t_n, w_n, v_n = (pltpu.roll(z, rows - 1, 0) for z in (t, w, v))
        flux = jnp.minimum(w, w_n) * (0.25 * (v + v_n) * (t + t_n) - 0.1 * (t_n - t))
        flux = jnp.where(row == rows - 1, 0.0, flux)
        flow = flow + (flux - pltpu.roll(flux, 1, 0))
        above = jnp.minimum(k + 1, levels - 1)
        upper = 0.2 * jnp.minimum(w, w_v[above]) * (t_v[above] - t)
        scale = 0.2 * m_v[k].astype(jnp.float32) / h_v[k]
        c_v[k] = scale
        out_v[k] = t + scale * ((upper - lower) - flow)
        return upper

    lax.fori_loop(0, levels, tracer_level, zero)

    arrived(f_v.at[:, high, all_columns], F_N)
    arrived(re.at[middle], P_E)
    arrived(rw.at[middle], P_W)
    arrived(re.at[high], P_NE)
    arrived(rw.at[high], P_NW)

    @pl.when(not_first)
    def _():
        arrived(f_v.at[:, low, all_columns], F_S)
        arrived(re.at[low], P_SE)
        arrived(rw.at[low], P_SW)

    @pl.when(first)
    def _():
        f_v[:, low, all_columns] = jnp.zeros((6, HALO, columns), jnp.float32)
        re[low] = jnp.zeros((HALO, 128), jnp.float32)
        rw[low] = jnp.zeros((HALO, 128), jnp.float32)

    @pl.when(last)
    def _():
        for f in range(6):
            old = f_v[f, high, all_columns]
            tiles = [old[:, c : c + 128] for c in range(columns - 128, -128, -128)]
            new = jnp.concatenate([flip_lanes(flip_rows(t), 127) for t in tiles], axis=1)
            f_v[f, high, all_columns] = new if f % 3 == 0 else -new
        field = lanes((HALO, 128)) // HALO
        even = (field == 0) | (field == 3)
        for ref in (re, rw):
            new = flip_lanes(flip_rows(ref[high]), HALO - 1)
            ref[high] = jnp.where(even, new, -new)

    ext = f_v.shape[1]
    lane = lanes((ext, 128))
    from_e, from_w = re[...], rw[...]
    for f in range(6):
        shift = (128 - HALO * f) % 128
        tile_e = pltpu.roll(from_e, shift, 1) if shift else from_e
        shift = 128 - HALO - HALO * f
        tile_w = pltpu.roll(from_w, shift, 1) if shift else from_w
        f_v[f, :, pl.ds(columns, 128)] = jnp.where(lane < 64, tile_e, tile_w)

    sent(f_v.at[:, own_high, all_columns], UP_F)

    @pl.when(not_first)
    def _():
        sent(f_v.at[:, own_low, all_columns], DN_F)

    d = f_v[3]
    a_v[0] = jnp.minimum(2.0 * d, 1.0)
    a_v[1] = 0.5 * jnp.minimum(d, pltpu.roll(d, wide - 1, 1))
    a_v[2] = 0.5 * jnp.minimum(d, pltpu.roll(d, ext - 1, 0))
    a_v[3] = 0.2 * f_v[4]
    a_v[4] = 0.2 * f_v[5]

    def cycles(span):
        count = span.size

        def step(_, carry):
            eta, ub, vb = (f_v[f, span, :] for f in range(3))
            wet = a_v[0, span, :]
            flux = a_v[1, span, :] * (ub + pltpu.roll(ub, wide - 1, 1))
            div = flux - pltpu.roll(flux, 1, 1)
            flux = a_v[2, span, :] * (vb + pltpu.roll(vb, count - 1, 0))
            div = div + (flux - pltpu.roll(flux, 1, 0))
            eta = eta - 0.2 * wet * div
            slope_x = pltpu.roll(eta, wide - 1, 1) - pltpu.roll(eta, 1, 1)
            slope_y = pltpu.roll(eta, count - 1, 0) - pltpu.roll(eta, 1, 0)
            f_v[0, span, :] = eta
            f_v[1, span, :] = wet * (ub - 0.05 * slope_x + a_v[3, span, :])
            f_v[2, span, :] = wet * (vb - 0.05 * slope_y + a_v[4, span, :])
            return carry

        lax.fori_loop(0, SUB // 2, step, 0)

    cycles(pl.ds(0, ext))
    cycles(pl.ds(SUB, ext - HALO))

    for f in range(3):
        o_st[f] = f_v[f, middle, all_columns]

    arrived(hn, T_N)
    arrived(se, T_E)
    arrived(sw, T_W)

    @pl.when(not_first)
    def _():
        arrived(hs, T_S)

    @pl.when(first)
    def _():
        hs[...] = jnp.zeros(hs.shape, jnp.float32)

    @pl.when(last)
    def _():
        for i in range(3):
            sign = -1.0 if i == 2 else 1.0
            old = hn[i]
            tiles = [old[:, c : c + 128] for c in range(columns - 128, -128, -128)]
            hn[i] = sign * jnp.concatenate([flip_lanes(t, 127) for t in tiles], axis=1)

    def face(t_a, t_b, w_a, w_b, u_a, u_b):
        return jnp.minimum(w_a, w_b) * (0.25 * (u_a + u_b) * (t_a + t_b) - 0.1 * (t_b - t_a))

    def packed_face(a, b):
        a_1, b_1 = pltpu.roll(a, 128 - levels, 1), pltpu.roll(b, 128 - levels, 1)
        a_2, b_2 = pltpu.roll(a, 128 - 2 * levels, 1), pltpu.roll(b, 128 - 2 * levels, 1)
        return face(a, b, a_1, b_1, a_2, b_2)

    flux_e = packed_face(qe[...], se[...])
    flux_w = packed_face(sw[...], qw[...])
    lane = lanes((rows, 128))
    for k in range(levels):
        edge = pl.ds(columns - 128, 128)
        moved = pltpu.roll(flux_e, 127 - k, 1)
        out_v[k, :, edge] = out_v[k, :, edge] - jnp.where(
            lane == 127, c_v[k, :, edge] * moved, 0.0
        )
        edge = pl.ds(0, 128)
        moved = pltpu.roll(flux_w, 128 - k, 1) if k else flux_w
        out_v[k, :, edge] = out_v[k, :, edge] + jnp.where(lane == 0, c_v[k, :, edge] * moved, 0.0)
    flux_n = face(gn[0], hn[0], gn[1], hn[1], gn[2], hn[2])
    out_v[:, rows - 1, :] = out_v[:, rows - 1, :] - c_v[:, rows - 1, :] * flux_n
    flux_s = face(hs[0], gs[0], hs[1], gs[1], hs[2], gs[2])
    out_v[:, 0, :] = out_v[:, 0, :] + c_v[:, 0, :] * flux_s

    sent(pe, SD_E)
    sent(pw, SD_W)
    sent(gn, SD_TU)
    sent(qe, SD_TE)
    sent(qw, SD_TW)

    @pl.when(not_last | jnp.logical_not(self_e))
    def _():
        sent(pe.at[part_high], SD_EU)

    @pl.when(not_last | jnp.logical_not(self_w))
    def _():
        sent(pw.at[part_high], SD_WU)

    @pl.when(not_first)
    def _():
        sent(pe.at[part_low], SD_ED)
        sent(pw.at[part_low], SD_WD)
        sent(gs, SD_TD)


def store_kernel(tr, st, o_tr, o_sf, o_zb, o_mb, sem):
    copies = [pltpu.make_async_copy(tr, o_tr, sem.at[3])]
    for f, dst in enumerate((o_sf, o_zb, o_mb)):
        copies.append(pltpu.make_async_copy(st.at[f], dst, sem.at[f]))
    for copy in copies:
        copy.start()
    for copy in copies:
        copy.wait()


def on_device(n_lat, n_lon, *args):
    levels, rows, columns = args[0].shape
    block = pltpu.VMEM((levels, rows, columns), jnp.float32)
    ext, wide = rows + 2 * HALO, columns + 128
    strip, long_strip = pltpu.VMEM((rows, 128), jnp.float32), pltpu.VMEM((ext, 128), jnp.float32)
    line = pltpu.VMEM((3, levels, columns), jnp.float32)
    flat = pltpu.VMEM((6, ext, wide), jnp.float32)
    scratch = [block, block, pltpu.VMEM((levels, rows, columns), jnp.int32)] + [block] * 4
    scratch += [flat] + [pltpu.VMEM((5, ext, wide), jnp.float32)]
    scratch += [strip] * 2 + [long_strip] * 2 + [strip] * 4 + [line] * 4
    scratch += [
        pltpu.SemaphoreType.DMA((8,)),
        pltpu.SemaphoreType.DMA((SLOTS,)), pltpu.SemaphoreType.DMA((SLOTS,)),
    ]
    whole = jax.ShapeDtypeStruct((levels, rows, columns), jnp.float32)
    surface = jax.ShapeDtypeStruct((rows, columns), jnp.float32)
    in_vmem = pl.BlockSpec(memory_space=pltpu.VMEM)
    anywhere = pl.BlockSpec(memory_space=pl.ANY)
    args = [pltpu.with_memory_space_constraint(a, pltpu.HBM) for a in args]
    tracer, state = pl.pallas_call(
        functools.partial(kernel, n_lat, n_lon),
        out_shape=(whole, jax.ShapeDtypeStruct((3, rows, columns), jnp.float32)),
        in_specs=[anywhere] * 8,
        out_specs=(in_vmem,) * 2,
        scratch_shapes=scratch,
        compiler_params=pltpu.CompilerParams(
            collective_id=0, has_side_effects=True, vmem_limit_bytes=32 << 20
        ),
        name="ocean",
    )(*args)
    return pl.pallas_call(
        store_kernel,
        out_shape=(whole, surface, surface, surface),
        in_specs=[in_vmem] * 2,
        out_specs=(anywhere,) * 4,
        scratch_shapes=[pltpu.SemaphoreType.DMA((4,))],
        compiler_params=pltpu.CompilerParams(vmem_limit_bytes=32 << 20),

        name="store",
    )(tracer, state)


def solution(mesh):
    whole, surface = P(None, "lat", "lon"), P("lat", "lon")
    return jax.shard_map(
        functools.partial(on_device, mesh.shape["lat"], mesh.shape["lon"]),
        mesh=mesh,
        in_specs=(whole,) * 5 + (surface,) * 3,
        out_specs=(whole, surface, surface, surface),
        check_vma=False,
    )
```

```python
import functools

import jax
import jax.numpy as jnp
from jax import lax
from jax.experimental import pallas as pl
from jax.experimental.pallas import tpu as pltpu
from jax.sharding import PartitionSpec as P

SUB = 8
HALO = 2 * SUB
RING = 8
PAD = 8
CHUNK = 8
MESH = pl.DeviceIdType.MESH

ST_N, ST_S, CF_N, CF_S = 0, 6, 12, 13
P_E, P_W, P_NE, P_SE, P_NW, P_SW = 14, 15, 16, 17, 18, 19
T_N, T_S, T_E, T_W = 20, 21, 22, 23
UP_ST, DN_ST, UP_CF, DN_CF = 0, 6, 12, 13
SD_E, SD_W, SD_EU, SD_ED, SD_WU, SD_WD = 14, 15, 16, 17, 18, 19
SD_TU, SD_TD, SD_TE, SD_TW = 20, 21, 22, 23
SLOTS = 24
N, S, E, W, NE, NW, SE, SW, FOLD, FOLD_E, FOLD_W = range(11)
OPPOSITE = (S, N, W, E, SW, SE, NW, NE, FOLD, FOLD_E, FOLD_W)


def lanes(shape):
    return lax.broadcasted_iota(jnp.int32, shape, 1)


def flip_rows(tile):
    rows = tile.shape[0]
    index = 7 - lax.broadcasted_iota(jnp.int32, (8, 128), 0)
    parts = [
        jnp.take_along_axis(tile[r : r + 8], index, axis=0) for r in range(rows - 8, -8, -8)
    ]
    return jnp.concatenate(parts, axis=0)


def flip_lanes(tile, mask):
    index = lanes((8, 128)) ^ mask
    parts = [
        jnp.take_along_axis(tile[r : r + 8], index, axis=1) for r in range(0, tile.shape[0], 8)
    ]
    return jnp.concatenate(parts, axis=0)


def kernel(
    n_lat, n_lon,
    tr, th, mk, zu, mv, sf, zb, mb,
    out_v, o_st,
    t_v, h_v, m_v, u_v, v_v, w_v, c_v,
    x_0, x_1, x_2, f_v, a_v, pe, pw, re, rw, qe, qw, se, sw, gn, gs, hn, hs,
    load_sem, send_sem, recv_sem, ready,
):
    levels, rows, columns = t_v.shape
    own_top = PAD + HALO
    top = own_top + rows
    ext = rows + 2 * HALO
    x_v = (x_0, x_1, x_2)
    lat, lon = lax.axis_index("lat"), lax.axis_index("lon")
    last, first = lat == n_lat - 1, lat == 0
    not_last, not_first = lat < n_lat - 1, lat > 0
    east, west = lax.rem(lon + 1, n_lon), lax.rem(lon + n_lon - 1, n_lon)
    mirror = n_lon - 1 - lon
    fold_e = lax.rem(2 * n_lon - 2 - lon, n_lon)
    fold_w = lax.rem(n_lon - lon, n_lon)

    low, own, high = pl.ds(PAD, HALO), pl.ds(own_top, rows), pl.ds(top, HALO)
    own_low, own_high = pl.ds(own_top, HALO), pl.ds(top - HALO, HALO)
    part_low, part_high = pl.ds(0, HALO), pl.ds(rows - HALO, HALO)
    edge_low, middle, edge_high = pl.ds(0, HALO), pl.ds(HALO, rows), pl.ds(HALO + rows, HALO)
    halves = (pl.ds(0, 128), pl.ds(128, 128))
    inner = pl.ds(0, 2)

    loads = [
        (th, h_v), (mk, m_v), (zu, u_v), (mv, v_v), (tr, t_v),
    ]
    for f, field in enumerate((sf, zb, mb)):
        for t in range(2):
            loads.append((field.at[:, halves[t]], x_v[f].at[t, own, :]))
    loads = [pltpu.make_async_copy(s, d, load_sem.at[i]) for i, (s, d) in enumerate(loads)]

    always = lat >= 0
    partners = {
        N: (lat + 1, lon, not_last),
        S: (lat - 1, lon, not_first),
        E: (lat, east, always),
        W: (lat, west, always),
        NE: (lat + 1, east, not_last),
        NW: (lat + 1, west, not_last),
        SE: (lat - 1, east, not_first),
        SW: (lat - 1, west, not_first),
        FOLD: (lat, mirror, last),
        FOLD_E: (lat, fold_e, last & (fold_e != lon)),
        FOLD_W: (lat, fold_w, last & (fold_w != lon)),
    }

    def order(some_lat, some_lon):
        ring = lax.rem(some_lat, RING)
        ring = jnp.where(ring < RING // 2, ring, RING + RING // 2 - 1 - ring)
        turn = lax.div(some_lat, RING)
        place = 4 * ring + 5 * turn + 13 * lax.div(some_lon, 2)
        near = 4 * (RING // 2) + 5 * ((n_lat - 1) // RING) + 13 * (n_lon // 4 - 1)
        far = (some_lat == n_lat - 1) & (some_lon >= n_lon // 2)
        return jnp.where(
            far, (near + 1) * n_lon + n_lon - 1 - some_lon, place * n_lon + some_lon
        )

    mine = order(lat, lon)
    later = {p: order(*at[:2]) > mine for p, at in partners.items()}

    def is_later(p):
        return partners[p][2] & later[p]

    def is_earlier(p):
        return partners[p][2] & jnp.logical_not(later[p])

    barrier = pltpu.get_barrier_semaphore()
    for p in (W, NW, SW, FOLD, FOLD_E, FOLD_W, N, S, E, NE, SE):

        @pl.when(is_later(p))
        def _():
            pl.semaphore_signal(
                barrier, inc=1, device_id=partners[p][:2], device_id_type=MESH
            )

    for load in loads:
        load.start()

    def send(src, dst, out_slot, in_slot, to_lat, to_lon):
        return pltpu.make_async_remote_copy(
            src_ref=src, dst_ref=dst, send_sem=send_sem.at[out_slot],
            recv_sem=recv_sem.at[in_slot], device_id=(to_lat, to_lon), device_id_type=MESH,
        )

    def arrived(dst, in_slot):
        send(dst, dst, 0, in_slot, lat, east).wait_recv()

    def sent(src, out_slot):
        send(src, src, out_slot, 0, lat, east).wait_send()


    state = (sf, zb, mb)

    def start(p, src, dst, out_slot, in_slot):
        send(src, dst, out_slot, in_slot, *partners[p][:2]).start()

    def send_state(p):
        rows_out = part_low if p == S else part_high
        rows_in = low if p == N else high
        out_slot, in_slot = DN_ST if p == S else UP_ST, ST_S if p == N else ST_N
        for f in range(3):
            for t in range(2):
                slot = 2 * f + t
                start(
                    p, state[f].at[rows_out, halves[t]], x_v[f].at[t, rows_in, :],
                    out_slot + slot, in_slot + slot,
                )

    def send_column(p):
        rows_out = own_low if p == S else own_high
        rows_in = low if p == N else high
        start(
            p, f_v.at[:, inner, rows_out, :], f_v.at[:, inner, rows_in, :],
            DN_CF if p == S else UP_CF, CF_S if p == N else CF_N,
        )

    sides = {
        E: (pe, rw.at[middle], SD_E, P_W),
        W: (pw, re.at[middle], SD_W, P_E),
        NE: (pe.at[part_high], rw.at[edge_low], SD_EU, P_SW),
        NW: (pw.at[part_high], re.at[edge_low], SD_WU, P_SE),
        SE: (pe.at[part_low], rw.at[edge_high], SD_ED, P_NW),
        SW: (pw.at[part_low], re.at[edge_high], SD_WD, P_NE),
        FOLD_E: (pe.at[part_high], re.at[edge_high], SD_EU, P_NE),
        FOLD_W: (pw.at[part_high], rw.at[edge_high], SD_WU, P_NW),
    }
    tracers = {
        N: (gn, hs, SD_TU, T_S),
        S: (gs, hn, SD_TD, T_N),
        E: (qe, sw, SD_TE, T_W),
        W: (qw, se, SD_TW, T_E),
        FOLD: (gn, hn, SD_TU, T_N),
    }

    def send_flat(p):
        if p in sides:
            start(p, *sides[p])
        else:
            send_column(p)

    def send_to_later(group):
        for p in group:

            @pl.when(is_later(p))
            def _():
                pl.semaphore_wait(ready.at[p], 1)
                if p not in sides:
                    send_state(p)
                send_flat(p)
                if p in tracers:
                    start(p, *tracers[p])

    count = sum(jnp.where(is_earlier(p), 1, 0) for p in partners)

    def greeted():
        @pl.when(count > 0)
        def _():
            pl.semaphore_wait(barrier, count)

        for p in (E, NE, SE, FOLD, FOLD_E, FOLD_W, W, NW, SW, S, N):

            @pl.when(is_earlier(p))
            def _():
                pl.semaphore_signal(
                    ready.at[OPPOSITE[p]], inc=1, device_id=partners[p][:2],
                    device_id_type=MESH,
                )

    @pl.when(last)
    def _():
        greeted()

        @pl.when(is_earlier(FOLD))
        def _():
            send_state(FOLD)

    for load in loads[:4]:
        load.wait()

    @pl.when(not_last)
    def _():
        greeted()

    for p in (N, S):

        @pl.when(is_earlier(p))
        def _():
            send_state(p)

    def add_level(k, sums):
        wet = m_v[k].astype(jnp.float32) * h_v[k]
        w_v[k] = wet
        return sums[0] + wet, sums[1] + wet * u_v[k], sums[2] + wet * v_v[k]

    zero = jnp.zeros((rows, columns), jnp.float32)
    depth, force_u, force_v = lax.fori_loop(0, levels, add_level, (zero, zero, zero))
    force_u, force_v = 0.05 * force_u, 0.05 * force_v
    for t in range(2):
        f_v[0, t, own, :] = depth[:, 128 * t : 128 * t + 128]
    for t in range(2):
        f_v[1, t, own, :] = force_u[:, 128 * t : 128 * t + 128]
    for t in range(2):
        f_v[2, t, own, :] = force_v[:, 128 * t : 128 * t + 128]

    for load in loads[4:]:
        load.wait()

    lane = lanes((rows, 128))
    firsts = [x_v[f][0, own, :] for f in range(3)]
    lasts = [x_v[f][1, own, :] for f in range(3)]
    for total in (depth, force_u, force_v):
        firsts.append(total[:, :128])
        lasts.append(total[:, columns - 128 :])
    pack_e = jnp.zeros((rows, 128), jnp.float32)
    pack_w = jnp.zeros((rows, 128), jnp.float32)
    for f in range(6):
        here = (lane >= HALO * f) & (lane < HALO * (f + 1))
        from_e = pltpu.roll(lasts[f], (HALO * f + HALO) % 128, 1)
        pack_e = jnp.where(here, from_e, pack_e)
        from_w = firsts[f]
        if f:
            from_w = pltpu.roll(from_w, HALO * f, 1)
        pack_w = jnp.where(here, from_w, pack_w)
    pe[...] = pack_e
    pw[...] = pack_w
    for p in (E, NE, SE, FOLD, S, N, FOLD_E, FOLD_W, W, NW, SW):

        @pl.when(is_earlier(p))
        def _():
            send_flat(p)

    @pl.when(last & (fold_e == lon))
    def _():
        pltpu.make_async_copy(pe.at[part_high], re.at[edge_high], recv_sem.at[P_NE]).start()

    @pl.when(last & (fold_w == lon))
    def _():
        pltpu.make_async_copy(pw.at[part_high], rw.at[edge_high], recv_sem.at[P_NW]).start()


    pack_e = jnp.zeros((rows, 128), jnp.float32)
    pack_w = jnp.zeros((rows, 128), jnp.float32)
    for i, source in enumerate((t_v, w_v, u_v)):
        for k in range(levels):
            slot = i * levels + k
            pack_e = jnp.where(
                lane == slot, pltpu.roll(source[k, :, columns - 128 :], slot + 1, 1), pack_e
            )
            from_w = source[k, :, :128]
            if slot:
                from_w = pltpu.roll(from_w, slot, 1)
            pack_w = jnp.where(lane == slot, from_w, pack_w)
    qe[...] = pack_e
    qw[...] = pack_w
    for i, source in enumerate((t_v, w_v, v_v)):
        gn[i] = source[:, rows - 1, :]
        gs[i] = source[:, 0, :]
    for p in (E, FOLD, S, N, W):

        @pl.when(is_earlier(p))
        def _():
            start(p, *tracers[p])

    send_to_later((N, S, E, NE, SE))

    col = lanes((rows, columns))
    row = lax.broadcasted_iota(jnp.int32, (rows, columns), 0)

    def tracer_level(k, lower):
        t, w, u, v = t_v[k], w_v[k], u_v[k], v_v[k]
        t_e, w_e, u_e = (pltpu.roll(z, columns - 1, 1) for z in (t, w, u))
        flux = jnp.minimum(w, w_e) * (0.25 * (u + u_e) * (t + t_e) - 0.1 * (t_e - t))
        flux = jnp.where(col == columns - 1, 0.0, flux)
        flow = flux - pltpu.roll(flux, 1, 1)
        t_n, w_n, v_n = (pltpu.roll(z, rows - 1, 0) for z in (t, w, v))
        flux = jnp.minimum(w, w_n) * (0.25 * (v + v_n) * (t + t_n) - 0.1 * (t_n - t))
        flux = jnp.where(row == rows - 1, 0.0, flux)
        flow = flow + (flux - pltpu.roll(flux, 1, 0))
        above = jnp.minimum(k + 1, levels - 1)
        upper = 0.2 * jnp.minimum(w, w_v[above]) * (t_v[above] - t)
        scale = 0.2 * m_v[k].astype(jnp.float32) / h_v[k]
        c_v[k] = scale
        out_v[k] = t + scale * ((upper - lower) - flow)
        return upper

    lax.fori_loop(0, levels, tracer_level, zero)
    send_to_later((W, NW, SW, FOLD, FOLD_E, FOLD_W))

    def face(t_a, t_b, w_a, w_b, u_a, u_b):
        return jnp.minimum(w_a, w_b) * (0.25 * (u_a + u_b) * (t_a + t_b) - 0.1 * (t_b - t_a))

    def packed_face(a, b):
        a_1, b_1 = pltpu.roll(a, 128 - levels, 1), pltpu.roll(b, 128 - levels, 1)
        a_2, b_2 = pltpu.roll(a, 128 - 2 * levels, 1), pltpu.roll(b, 128 - 2 * levels, 1)
        return face(a, b, a_1, b_1, a_2, b_2)

    lane = lanes((rows, 128))
    arrived(se, T_E)

    @pl.when(not_first)
    def _():
        arrived(hs, T_S)

    @pl.when(first)
    def _():
        hs[...] = jnp.zeros(hs.shape, jnp.float32)

    flux_e = packed_face(qe[...], se[...])
    for k in range(levels):
        edge = halves[1]
        moved = pltpu.roll(flux_e, 127 - k, 1)
        out_v[k, :, edge] = out_v[k, :, edge] - jnp.where(
            lane == 127, c_v[k, :, edge] * moved, 0.0
        )
    flux_s = face(hs[0], gs[0], hs[1], gs[1], hs[2], gs[2])
    out_v[:, 0, :] = out_v[:, 0, :] + c_v[:, 0, :] * flux_s

    for f in range(3):
        for t in range(2):
            arrived(x_v[f].at[t, high, :], ST_N + 2 * f + t)
    arrived(f_v.at[:, inner, high, :], CF_N)
    arrived(re.at[middle], P_E)
    arrived(rw.at[middle], P_W)
    arrived(re.at[edge_high], P_NE)
    arrived(rw.at[edge_high], P_NW)

    @pl.when(not_first)
    def _():
        for f in range(3):
            for t in range(2):
                arrived(x_v[f].at[t, low, :], ST_S + 2 * f + t)
        arrived(f_v.at[:, inner, low, :], CF_S)
        arrived(re.at[edge_low], P_SE)
        arrived(rw.at[edge_low], P_SW)

    @pl.when(first)
    def _():
        f_v[:, inner, low, :] = jnp.zeros((3, 2, HALO, 128), jnp.float32)
        for f in range(3):
            x_v[f][inner, low, :] = jnp.zeros((2, HALO, 128), jnp.float32)
        re[edge_low] = jnp.zeros((HALO, 128), jnp.float32)
        rw[edge_low] = jnp.zeros((HALO, 128), jnp.float32)

    @pl.when(last)
    def _():
        for f in range(6):
            ref = x_v[f] if f < 3 else f_v.at[f - 3]
            old = [ref[t, high, :] for t in range(2)]
            for t in range(2):
                new = flip_lanes(flip_rows(old[1 - t]), 127)
                ref[t, high, :] = new if f % 3 == 0 else -new
        field = lanes((HALO, 128)) // HALO
        even = (field == 0) | (field == 3)
        for ref in (re, rw):
            new = flip_lanes(flip_rows(ref[edge_high]), HALO - 1)
            ref[edge_high] = jnp.where(even, new, -new)

    span = pl.ds(PAD, ext)
    lane = lanes((ext, 128))
    from_e, from_w = re[...], rw[...]
    for f in range(6):
        shift = (128 - HALO * f) % 128
        tile_e = pltpu.roll(from_e, shift, 1) if shift else from_e
        shift = 128 - HALO - HALO * f
        tile_w = pltpu.roll(from_w, shift, 1) if shift else from_w
        ref = x_v[f] if f < 3 else f_v.at[f - 3]
        ref[2, span, :] = jnp.where(lane < 64, tile_e, tile_w)

    def to_east_of(tiles):
        turned = [pltpu.roll(x, 127, 1) for x in tiles]
        edge = lanes(tiles[0].shape) == 127
        return [jnp.where(edge, turned[(t + 1) % 3], turned[t]) for t in range(3)]

    def to_west_of(tiles):
        turned = [pltpu.roll(x, 1, 1) for x in tiles]
        edge = lanes(tiles[0].shape) == 0
        return [jnp.where(edge, turned[(t + 2) % 3], turned[t]) for t in range(3)]

    for r in range(PAD, PAD + ext, HALO):
        here, north = pl.ds(r, HALO), pl.ds(r + 1, HALO)
        d = [f_v[0, t, here, :] for t in range(3)]
        d_e, d_w = to_east_of(d), to_west_of(d)
        for t in range(3):
            wet = jnp.minimum(2.0 * d[t], 1.0)
            a_v[0, t, here, :] = wet
            a_v[1, t, here, :] = 0.01 * wet
            a_v[2, t, here, :] = 0.5 * jnp.minimum(d[t], d_e[t])
            a_v[6, t, here, :] = 0.5 * jnp.minimum(d[t], d_w[t])
            a_v[3, t, here, :] = 0.5 * jnp.minimum(d[t], f_v[0, t, north, :])
            a_v[4, t, here, :] = 0.2 * f_v[1, t, here, :]
            a_v[5, t, here, :] = 0.2 * f_v[2, t, here, :]
            x_v[0][t, here, :] = 0.05 * x_v[0][t, here, :]

    def heights(r):
        here, north, south = pl.ds(r, CHUNK), pl.ds(r + 1, CHUNK), pl.ds(r - 1, CHUNK)
        ub = [x_1[t, here, :] for t in range(3)]
        ub_e, ub_w = to_east_of(ub), to_west_of(ub)
        for t in range(3):
            vb = x_2[t, here, :]
            out_n = a_v[3, t, here, :] * (vb + x_2[t, north, :])
            in_s = a_v[3, t, south, :] * (vb + x_2[t, south, :])
            out_e = a_v[2, t, here, :] * (ub[t] + ub_e[t])
            in_w = a_v[6, t, here, :] * (ub[t] + ub_w[t])
            div = (out_e - in_w) + (out_n - in_s)
            x_0[t, here, :] = x_0[t, here, :] - a_v[1, t, here, :] * div

    def speeds(r):
        here, north, south = pl.ds(r, CHUNK), pl.ds(r + 1, CHUNK), pl.ds(r - 1, CHUNK)
        eta = [x_0[t, here, :] for t in range(3)]
        eta_e, eta_w = to_east_of(eta), to_west_of(eta)
        for t in range(3):
            wet = a_v[0, t, here, :]
            drive = a_v[4, t, here, :] - (eta_e[t] - eta_w[t])
            x_1[t, here, :] = wet * (x_1[t, here, :] + drive)
            slope = x_0[t, north, :] - x_0[t, south, :]
            drive = a_v[5, t, here, :] - slope
            x_2[t, here, :] = wet * (x_2[t, here, :] + drive)

    def cycles(start_row, count):
        def step(_, carry):
            for r in range(start_row, start_row + count, CHUNK):
                heights(r)
                if r > start_row:
                    speeds(r - CHUNK)
            speeds(start_row + count - CHUNK)
            return carry

        lax.fori_loop(0, SUB // 2, step, 0, unroll=True)

    cycles(PAD, ext)
    cycles(PAD + SUB, ext - HALO)
    for t in range(2):
        o_st[0, :, halves[t]] = 20.0 * x_v[0][t, own, :]
        for f in range(1, 3):
            o_st[f, :, halves[t]] = x_v[f][t, own, :]

    arrived(hn, T_N)
    arrived(sw, T_W)

    @pl.when(last)
    def _():
        for i in range(3):
            old = hn[i]
            tiles = [old[:, c : c + 128] for c in range(columns - 128, -128, -128)]
            new = jnp.concatenate([flip_lanes(t, 127) for t in tiles], axis=1)
            hn[i] = -new if i == 2 else new

    flux_w = packed_face(sw[...], qw[...])
    for k in range(levels):
        edge = halves[0]
        moved = pltpu.roll(flux_w, 128 - k, 1) if k else flux_w
        out_v[k, :, edge] = out_v[k, :, edge] + jnp.where(
            lanes((rows, 128)) == 0, c_v[k, :, edge] * moved, 0.0
        )
    flux_n = face(gn[0], hn[0], gn[1], hn[1], gn[2], hn[2])
    out_v[:, rows - 1, :] = out_v[:, rows - 1, :] - c_v[:, rows - 1, :] * flux_n

    for slot in range(6):
        sent(sf.at[part_low, halves[0]], UP_ST + slot)
    sent(f_v.at[:, inner, own_low, :], UP_CF)
    sent(pe, SD_E)
    sent(pw, SD_W)
    sent(gn, SD_TU)
    sent(qe, SD_TE)
    sent(qw, SD_TW)

    @pl.when(not_last | (fold_e != lon))
    def _():
        sent(pe.at[part_high], SD_EU)

    @pl.when(not_last | (fold_w != lon))
    def _():
        sent(pw.at[part_high], SD_WU)

    @pl.when(not_first)
    def _():
        for slot in range(6):
            sent(sf.at[part_low, halves[0]], DN_ST + slot)
        sent(f_v.at[:, inner, own_low, :], DN_CF)
        sent(pe.at[part_low], SD_ED)
        sent(pw.at[part_low], SD_WD)
        sent(gs, SD_TD)


def store_kernel(tr, st, o_tr, o_sf, o_zb, o_mb, sem):
    copies = [pltpu.make_async_copy(tr, o_tr, sem.at[3])]
    for f, dst in enumerate((o_sf, o_zb, o_mb)):
        copies.append(pltpu.make_async_copy(st.at[f], dst, sem.at[f]))
    for copy in copies:
        copy.start()
    for copy in copies:
        copy.wait()


def on_device(n_lat, n_lon, *args):
    levels, rows, columns = args[0].shape
    block = pltpu.VMEM((levels, rows, columns), jnp.float32)
    ext, wide = rows + 2 * HALO, columns // 128 + 1
    strip, long_strip = pltpu.VMEM((rows, 128), jnp.float32), pltpu.VMEM((ext, 128), jnp.float32)
    line = pltpu.VMEM((3, levels, columns), jnp.float32)
    tiles = (wide, ext + 2 * PAD, 128)
    scratch = [block, block, pltpu.VMEM((levels, rows, columns), jnp.int32)] + [block] * 4
    scratch += [pltpu.VMEM(tiles, jnp.float32)] * 3
    scratch += [pltpu.VMEM((n, *tiles), jnp.float32) for n in (3, 7)]
    scratch += [strip] * 2 + [long_strip] * 2 + [strip] * 4 + [line] * 4
    scratch += [
        pltpu.SemaphoreType.DMA((11,)),
        pltpu.SemaphoreType.DMA((SLOTS,)), pltpu.SemaphoreType.DMA((SLOTS,)),
        pltpu.SemaphoreType.REGULAR((11,)),
    ]
    whole = jax.ShapeDtypeStruct((levels, rows, columns), jnp.float32)
    surface = jax.ShapeDtypeStruct((rows, columns), jnp.float32)
    in_vmem = pl.BlockSpec(memory_space=pltpu.VMEM)
    anywhere = pl.BlockSpec(memory_space=pl.ANY)
    args = [pltpu.with_memory_space_constraint(a, pltpu.HBM) for a in args]
    tracer, state = pl.pallas_call(
        functools.partial(kernel, n_lat, n_lon),
        out_shape=(whole, jax.ShapeDtypeStruct((3, rows, columns), jnp.float32)),
        in_specs=[anywhere] * 8,
        out_specs=(in_vmem,) * 2,
        scratch_shapes=scratch,
        compiler_params=pltpu.CompilerParams(
            collective_id=0, has_side_effects=True, vmem_limit_bytes=32 << 20
        ),
        name="ocean",
    )(*args)
    return pl.pallas_call(
        store_kernel,
        out_shape=(whole, surface, surface, surface),
        in_specs=[in_vmem] * 2,
        out_specs=(anywhere,) * 4,
        scratch_shapes=[pltpu.SemaphoreType.DMA((4,))],
        compiler_params=pltpu.CompilerParams(vmem_limit_bytes=32 << 20),

        name="store",
    )(tracer, state)


def solution(mesh):
    whole, surface = P(None, "lat", "lon"), P("lat", "lon")
    return jax.shard_map(
        functools.partial(on_device, mesh.shape["lat"], mesh.shape["lon"]),
        mesh=mesh,
        in_specs=(whole,) * 5 + (surface,) * 3,
        out_specs=(whole, surface, surface, surface),
        check_vma=False,
    )
```

```python
import functools

import jax
import jax.numpy as jnp
from jax import lax
from jax.experimental import pallas as pl
from jax.experimental.pallas import tpu as pltpu
from jax.sharding import PartitionSpec as P

SUB = 8
HALO = 2 * SUB
RING = 8
PAD = 8
CHUNK = 8
MESH = pl.DeviceIdType.MESH

ST_N, ST_S, CF_N, CF_S = 0, 6, 12, 13
P_E, P_W, P_NE, P_SE, P_NW, P_SW = 14, 15, 16, 17, 18, 19
T_N, T_S, T_E, T_W = 20, 21, 22, 23
UP_ST, DN_ST, UP_CF, DN_CF = 0, 6, 12, 13
SD_E, SD_W, SD_EU, SD_ED, SD_WU, SD_WD = 14, 15, 16, 17, 18, 19
SD_TU, SD_TD, SD_TE, SD_TW = 20, 21, 22, 23
SLOTS = 24
N, S, E, W, NE, NW, SE, SW, FOLD, FOLD_E, FOLD_W = range(11)
OPPOSITE = (S, N, W, E, SW, SE, NW, NE, FOLD, FOLD_E, FOLD_W)


def lanes(shape):
    return lax.broadcasted_iota(jnp.int32, shape, 1)


def flip_rows(tile):
    rows = tile.shape[0]
    index = 7 - lax.broadcasted_iota(jnp.int32, (8, 128), 0)
    parts = [
        jnp.take_along_axis(tile[r : r + 8], index, axis=0) for r in range(rows - 8, -8, -8)
    ]
    return jnp.concatenate(parts, axis=0)


def flip_lanes(tile, mask):
    index = lanes((8, 128)) ^ mask
    parts = [
        jnp.take_along_axis(tile[r : r + 8], index, axis=1) for r in range(0, tile.shape[0], 8)
    ]
    return jnp.concatenate(parts, axis=0)


def kernel(
    n_lat, n_lon,
    tr, th, mk, zu, mv, sf, zb, mb,
    out_v, o_st,
    t_v, h_v, m_v, u_v, v_v, w_v, c_v,
    x_0, x_1, x_2, f_v, a_v, pe, pw, re, rw, qe, qw, se, sw, gn, gs, hn, hs,
    load_sem, send_sem, recv_sem, ready,
):
    levels, rows, columns = t_v.shape
    own_top = PAD + HALO
    top = own_top + rows
    ext = rows + 2 * HALO
    x_v = (x_0, x_1, x_2)
    lat, lon = lax.axis_index("lat"), lax.axis_index("lon")
    last, first = lat == n_lat - 1, lat == 0
    not_last, not_first = lat < n_lat - 1, lat > 0
    east, west = lax.rem(lon + 1, n_lon), lax.rem(lon + n_lon - 1, n_lon)
    mirror = n_lon - 1 - lon
    fold_e = lax.rem(2 * n_lon - 2 - lon, n_lon)
    fold_w = lax.rem(n_lon - lon, n_lon)

    low, own, high = pl.ds(PAD, HALO), pl.ds(own_top, rows), pl.ds(top, HALO)
    own_low, own_high = pl.ds(own_top, HALO), pl.ds(top - HALO, HALO)
    part_low, part_high = pl.ds(0, HALO), pl.ds(rows - HALO, HALO)
    edge_low, middle, edge_high = pl.ds(0, HALO), pl.ds(HALO, rows), pl.ds(HALO + rows, HALO)
    halves = (pl.ds(0, 128), pl.ds(128, 128))
    inner = pl.ds(0, 2)

    loads = [
        (th, h_v), (mk, m_v), (zu, u_v), (mv, v_v), (tr, t_v),
    ]
    for f, field in enumerate((sf, zb, mb)):
        for t in range(2):
            loads.append((field.at[:, halves[t]], x_v[f].at[t, own, :]))
    loads = [pltpu.make_async_copy(s, d, load_sem.at[i]) for i, (s, d) in enumerate(loads)]

    always = lat >= 0
    partners = {
        N: (lat + 1, lon, not_last),
        S: (lat - 1, lon, not_first),
        E: (lat, east, always),
        W: (lat, west, always),
        NE: (lat + 1, east, not_last),
        NW: (lat + 1, west, not_last),
        SE: (lat - 1, east, not_first),
        SW: (lat - 1, west, not_first),
        FOLD: (lat, mirror, last),
        FOLD_E: (lat, fold_e, last & (fold_e != lon)),
        FOLD_W: (lat, fold_w, last & (fold_w != lon)),
    }

    def order(some_lat, some_lon):
        ring = lax.rem(some_lat, RING)
        ring = jnp.where(ring < RING // 2, ring, RING + RING // 2 - 1 - ring)
        turn = lax.div(some_lat, RING)
        place = 4 * ring + 5 * turn + 13 * lax.div(some_lon, 2)
        near = 4 * (RING // 2) + 5 * ((n_lat - 1) // RING) + 13 * (n_lon // 4 - 1)
        far = (some_lat == n_lat - 1) & (some_lon >= n_lon // 2)
        swapped = some_lon + 1 - 2 * lax.rem(some_lon, 2)
        return jnp.where(far, near + 1, place) * n_lon + swapped

    mine = order(lat, lon)
    later = {p: order(*at[:2]) > mine for p, at in partners.items()}

    def is_later(p):
        return partners[p][2] & later[p]

    def is_earlier(p):
        return partners[p][2] & jnp.logical_not(later[p])

    barrier = pltpu.get_barrier_semaphore()
    for p in (W, NW, SW, FOLD, FOLD_E, FOLD_W, N, S, E, NE, SE):

        @pl.when(is_later(p))
        def _():
            pl.semaphore_signal(
                barrier, inc=1, device_id=partners[p][:2], device_id_type=MESH
            )

    for load in loads:
        load.start()

    def send(src, dst, out_slot, in_slot, to_lat, to_lon):
        return pltpu.make_async_remote_copy(
            src_ref=src, dst_ref=dst, send_sem=send_sem.at[out_slot],
            recv_sem=recv_sem.at[in_slot], device_id=(to_lat, to_lon), device_id_type=MESH,
        )

    def arrived(dst, in_slot):
        send(dst, dst, 0, in_slot, lat, east).wait_recv()

    def sent(src, out_slot):
        send(src, src, out_slot, 0, lat, east).wait_send()


    state = (sf, zb, mb)

    def start(p, src, dst, out_slot, in_slot):
        send(src, dst, out_slot, in_slot, *partners[p][:2]).start()

    def send_state(p):
        rows_out = part_low if p == S else part_high
        rows_in = low if p == N else high
        out_slot, in_slot = DN_ST if p == S else UP_ST, ST_S if p == N else ST_N
        for f in range(3):
            for t in range(2):
                slot = 2 * f + t
                start(
                    p, state[f].at[rows_out, halves[t]], x_v[f].at[t, rows_in, :],
                    out_slot + slot, in_slot + slot,
                )

    def send_column(p):
        rows_out = own_low if p == S else own_high
        rows_in = low if p == N else high
        start(
            p, f_v.at[:, inner, rows_out, :], f_v.at[:, inner, rows_in, :],
            DN_CF if p == S else UP_CF, CF_S if p == N else CF_N,
        )

    sides = {
        E: (pe, rw.at[middle], SD_E, P_W),
        W: (pw, re.at[middle], SD_W, P_E),
        NE: (pe.at[part_high], rw.at[edge_low], SD_EU, P_SW),
        NW: (pw.at[part_high], re.at[edge_low], SD_WU, P_SE),
        SE: (pe.at[part_low], rw.at[edge_high], SD_ED, P_NW),
        SW: (pw.at[part_low], re.at[edge_high], SD_WD, P_NE),
        FOLD_E: (pe.at[part_high], re.at[edge_high], SD_EU, P_NE),
        FOLD_W: (pw.at[part_high], rw.at[edge_high], SD_WU, P_NW),
    }
    tracers = {
        N: (gn, hs, SD_TU, T_S),
        S: (gs, hn, SD_TD, T_N),
        E: (qe, sw, SD_TE, T_W),
        W: (qw, se, SD_TW, T_E),
        FOLD: (gn, hn, SD_TU, T_N),
    }

    def send_flat(p):
        if p in sides:
            start(p, *sides[p])
        else:
            send_column(p)

    def send_to_later(group):
        for p in group:

            @pl.when(is_later(p))
            def _():
                pl.semaphore_wait(ready.at[p], 1)
                if p not in sides:
                    send_state(p)
                send_flat(p)
                if p in tracers:
                    start(p, *tracers[p])

    count = sum(jnp.where(is_earlier(p), 1, 0) for p in partners)

    def greeted():
        @pl.when(count > 0)
        def _():
            pl.semaphore_wait(barrier, count)

        for p in (E, NE, SE, FOLD, FOLD_E, FOLD_W, W, NW, SW, S, N):

            @pl.when(is_earlier(p))
            def _():
                pl.semaphore_signal(
                    ready.at[OPPOSITE[p]], inc=1, device_id=partners[p][:2],
                    device_id_type=MESH,
                )

    @pl.when(last)
    def _():
        greeted()

        @pl.when(is_earlier(FOLD))
        def _():
            send_state(FOLD)

    in_front = lax.div(mirror, 2) != 1

    for load in loads[:4]:
        load.wait()

    @pl.when(not_last)
    def _():
        greeted()

    for p in (N, S):

        @pl.when(is_earlier(p))
        def _():
            send_state(p)

    def add_level(k, sums):
        wet = m_v[k].astype(jnp.float32) * h_v[k]
        w_v[k] = wet
        return sums[0] + wet, sums[1] + wet * u_v[k], sums[2] + wet * v_v[k]

    zero = jnp.zeros((rows, columns), jnp.float32)
    depth, force_u, force_v = lax.fori_loop(0, levels, add_level, (zero, zero, zero))
    force_u, force_v = 0.05 * force_u, 0.05 * force_v
    for t in range(2):
        f_v[0, t, own, :] = depth[:, 128 * t : 128 * t + 128]
    for t in range(2):
        f_v[1, t, own, :] = force_u[:, 128 * t : 128 * t + 128]
    for t in range(2):
        f_v[2, t, own, :] = force_v[:, 128 * t : 128 * t + 128]

    for load in loads[4:]:
        load.wait()

    @pl.when(is_earlier(FOLD) & in_front)
    def _():
        send_column(FOLD)

    lane = lanes((rows, 128))
    firsts = [x_v[f][0, own, :] for f in range(3)]
    lasts = [x_v[f][1, own, :] for f in range(3)]
    for total in (depth, force_u, force_v):
        firsts.append(total[:, :128])
        lasts.append(total[:, columns - 128 :])
    pack_e = jnp.zeros((rows, 128), jnp.float32)
    pack_w = jnp.zeros((rows, 128), jnp.float32)
    for f in range(6):
        here = (lane >= HALO * f) & (lane < HALO * (f + 1))
        from_e = pltpu.roll(lasts[f], (HALO * f + HALO) % 128, 1)
        pack_e = jnp.where(here, from_e, pack_e)
        from_w = firsts[f]
        if f:
            from_w = pltpu.roll(from_w, HALO * f, 1)
        pack_w = jnp.where(here, from_w, pack_w)
    pe[...] = pack_e
    pw[...] = pack_w
    for p in (E, NE, SE, FOLD_E, FOLD_W, W, NW, SW):

        @pl.when(is_earlier(p))
        def _():
            start(p, *sides[p])

    for p in (S, N):

        @pl.when(is_earlier(p))
        def _():
            send_column(p)

    @pl.when(last & (fold_e == lon))
    def _():
        pltpu.make_async_copy(pe.at[part_high], re.at[edge_high], recv_sem.at[P_NE]).start()

    @pl.when(last & (fold_w == lon))
    def _():
        pltpu.make_async_copy(pw.at[part_high], rw.at[edge_high], recv_sem.at[P_NW]).start()


    pack_e = jnp.zeros((rows, 128), jnp.float32)
    pack_w = jnp.zeros((rows, 128), jnp.float32)
    for i, source in enumerate((t_v, w_v, u_v)):
        for k in range(levels):
            slot = i * levels + k
            pack_e = jnp.where(
                lane == slot, pltpu.roll(source[k, :, columns - 128 :], slot + 1, 1), pack_e
            )
            from_w = source[k, :, :128]
            if slot:
                from_w = pltpu.roll(from_w, slot, 1)
            pack_w = jnp.where(lane == slot, from_w, pack_w)
    qe[...] = pack_e
    qw[...] = pack_w
    for i, source in enumerate((t_v, w_v, v_v)):
        gn[i] = source[:, rows - 1, :]
        gs[i] = source[:, 0, :]
    for p in (E, FOLD, S, N, W):
        now = is_earlier(p) & in_front if p == FOLD else is_earlier(p)

        @pl.when(now)
        def _():
            start(p, *tracers[p])

    send_to_later((N, S, E, NE, SE))

    col = lanes((rows, columns))
    row = lax.broadcasted_iota(jnp.int32, (rows, columns), 0)

    def tracer_level(k, lower):
        t, w, u, v = t_v[k], w_v[k], u_v[k], v_v[k]
        t_e, w_e, u_e = (pltpu.roll(z, columns - 1, 1) for z in (t, w, u))
        flux = jnp.minimum(w, w_e) * (0.25 * (u + u_e) * (t + t_e) - 0.1 * (t_e - t))
        flux = jnp.where(col == columns - 1, 0.0, flux)
        flow = flux - pltpu.roll(flux, 1, 1)
        t_n, w_n, v_n = (pltpu.roll(z, rows - 1, 0) for z in (t, w, v))
        flux = jnp.minimum(w, w_n) * (0.25 * (v + v_n) * (t + t_n) - 0.1 * (t_n - t))
        flux = jnp.where(row == rows - 1, 0.0, flux)
        flow = flow + (flux - pltpu.roll(flux, 1, 0))
        above = jnp.minimum(k + 1, levels - 1)
        upper = 0.2 * jnp.minimum(w, w_v[above]) * (t_v[above] - t)
        scale = 0.2 * m_v[k].astype(jnp.float32) / h_v[k]
        c_v[k] = scale
        out_v[k] = t + scale * ((upper - lower) - flow)
        return upper

    lax.fori_loop(0, levels, tracer_level, zero)

    @pl.when(is_earlier(FOLD) & jnp.logical_not(in_front))
    def _():
        send_column(FOLD)
        start(FOLD, *tracers[FOLD])

    send_to_later((FOLD, FOLD_E, FOLD_W, W, NW, SW))

    def face(t_a, t_b, w_a, w_b, u_a, u_b):
        return jnp.minimum(w_a, w_b) * (0.25 * (u_a + u_b) * (t_a + t_b) - 0.1 * (t_b - t_a))

    def packed_face(a, b):
        a_1, b_1 = pltpu.roll(a, 128 - levels, 1), pltpu.roll(b, 128 - levels, 1)
        a_2, b_2 = pltpu.roll(a, 128 - 2 * levels, 1), pltpu.roll(b, 128 - 2 * levels, 1)
        return face(a, b, a_1, b_1, a_2, b_2)

    lane = lanes((rows, 128))
    arrived(se, T_E)

    @pl.when(not_first)
    def _():
        arrived(hs, T_S)

    @pl.when(first)
    def _():
        hs[...] = jnp.zeros(hs.shape, jnp.float32)

    flux_e = packed_face(qe[...], se[...])
    for k in range(levels):
        edge = halves[1]
        moved = pltpu.roll(flux_e, 127 - k, 1)
        out_v[k, :, edge] = out_v[k, :, edge] - jnp.where(
            lane == 127, c_v[k, :, edge] * moved, 0.0
        )
    flux_s = face(hs[0], gs[0], hs[1], gs[1], hs[2], gs[2])
    out_v[:, 0, :] = out_v[:, 0, :] + c_v[:, 0, :] * flux_s

    for f in range(3):
        for t in range(2):
            arrived(x_v[f].at[t, high, :], ST_N + 2 * f + t)

    def flip_north(refs):
        for f, ref in enumerate(refs):
            old = [ref[t, high, :] for t in range(2)]
            for t in range(2):
                new = flip_lanes(flip_rows(old[1 - t]), 127)
                ref[t, high, :] = new if f == 0 else -new

    @pl.when(last)
    def _():
        flip_north(x_v)

    arrived(f_v.at[:, inner, high, :], CF_N)
    arrived(re.at[middle], P_E)
    arrived(rw.at[middle], P_W)
    arrived(re.at[edge_high], P_NE)
    arrived(rw.at[edge_high], P_NW)

    @pl.when(not_first)
    def _():
        for f in range(3):
            for t in range(2):
                arrived(x_v[f].at[t, low, :], ST_S + 2 * f + t)
        arrived(f_v.at[:, inner, low, :], CF_S)
        arrived(re.at[edge_low], P_SE)
        arrived(rw.at[edge_low], P_SW)

    @pl.when(first)
    def _():
        f_v[:, inner, low, :] = jnp.zeros((3, 2, HALO, 128), jnp.float32)
        for f in range(3):
            x_v[f][inner, low, :] = jnp.zeros((2, HALO, 128), jnp.float32)
        re[edge_low] = jnp.zeros((HALO, 128), jnp.float32)
        rw[edge_low] = jnp.zeros((HALO, 128), jnp.float32)

    @pl.when(last)
    def _():
        flip_north([f_v.at[f] for f in range(3)])
        field = lanes((HALO, 128)) // HALO
        even = (field == 0) | (field == 3)
        for ref in (re, rw):
            new = flip_lanes(flip_rows(ref[edge_high]), HALO - 1)
            ref[edge_high] = jnp.where(even, new, -new)

    span = pl.ds(PAD, ext)
    lane = lanes((ext, 128))
    from_e, from_w = re[...], rw[...]
    for f in range(6):
        shift = (128 - HALO * f) % 128
        tile_e = pltpu.roll(from_e, shift, 1) if shift else from_e
        shift = 128 - HALO - HALO * f
        tile_w = pltpu.roll(from_w, shift, 1) if shift else from_w
        ref = x_v[f] if f < 3 else f_v.at[f - 3]
        ref[2, span, :] = jnp.where(lane < 64, tile_e, tile_w)

    def to_east_of(tiles):
        turned = [pltpu.roll(x, 127, 1) for x in tiles]
        edge = lanes(tiles[0].shape) == 127
        return [jnp.where(edge, turned[(t + 1) % 3], turned[t]) for t in range(3)]

    def to_west_of(tiles):
        turned = [pltpu.roll(x, 1, 1) for x in tiles]
        edge = lanes(tiles[0].shape) == 0
        return [jnp.where(edge, turned[(t + 2) % 3], turned[t]) for t in range(3)]

    for r in range(PAD, PAD + ext, HALO):
        here, north = pl.ds(r, HALO), pl.ds(r + 1, HALO)
        d = [f_v[0, t, here, :] for t in range(3)]
        d_e, d_w = to_east_of(d), to_west_of(d)
        for t in range(3):
            wet = jnp.minimum(2.0 * d[t], 1.0)
            a_v[0, t, here, :] = wet
            a_v[1, t, here, :] = 0.01 * wet
            a_v[2, t, here, :] = 0.5 * jnp.minimum(d[t], d_e[t])
            a_v[6, t, here, :] = 0.5 * jnp.minimum(d[t], d_w[t])
            a_v[3, t, here, :] = 0.5 * jnp.minimum(d[t], f_v[0, t, north, :])
            a_v[4, t, here, :] = 0.2 * f_v[1, t, here, :]
            a_v[5, t, here, :] = 0.2 * f_v[2, t, here, :]
            x_v[0][t, here, :] = 0.05 * x_v[0][t, here, :]

    def heights(r):
        here, north, south = pl.ds(r, CHUNK), pl.ds(r + 1, CHUNK), pl.ds(r - 1, CHUNK)
        ub = [x_1[t, here, :] for t in range(3)]
        ub_e, ub_w = to_east_of(ub), to_west_of(ub)
        for t in range(3):
            vb = x_2[t, here, :]
            out_n = a_v[3, t, here, :] * (vb + x_2[t, north, :])
            in_s = a_v[3, t, south, :] * (vb + x_2[t, south, :])
            out_e = a_v[2, t, here, :] * (ub[t] + ub_e[t])
            in_w = a_v[6, t, here, :] * (ub[t] + ub_w[t])
            div = (out_e - in_w) + (out_n - in_s)
            x_0[t, here, :] = x_0[t, here, :] - a_v[1, t, here, :] * div

    def speeds(r):
        here, north, south = pl.ds(r, CHUNK), pl.ds(r + 1, CHUNK), pl.ds(r - 1, CHUNK)
        eta = [x_0[t, here, :] for t in range(3)]
        eta_e, eta_w = to_east_of(eta), to_west_of(eta)
        for t in range(3):
            wet = a_v[0, t, here, :]
            drive = a_v[4, t, here, :] - (eta_e[t] - eta_w[t])
            x_1[t, here, :] = wet * (x_1[t, here, :] + drive)
            slope = x_0[t, north, :] - x_0[t, south, :]
            drive = a_v[5, t, here, :] - slope
            x_2[t, here, :] = wet * (x_2[t, here, :] + drive)

    def cycles(start_row, count):
        def step(_, carry):
            for r in range(start_row, start_row + count, CHUNK):
                heights(r)
                if r > start_row:
                    speeds(r - CHUNK)
            speeds(start_row + count - CHUNK)
            return carry

        lax.fori_loop(0, SUB // 2, step, 0, unroll=True)

    cycles(PAD, ext)
    cycles(PAD + SUB, ext - HALO)
    for t in range(2):
        o_st[0, :, halves[t]] = 20.0 * x_v[0][t, own, :]
        for f in range(1, 3):
            o_st[f, :, halves[t]] = x_v[f][t, own, :]

    arrived(hn, T_N)
    arrived(sw, T_W)

    @pl.when(last)
    def _():
        for i in range(3):
            old = hn[i]
            tiles = [old[:, c : c + 128] for c in range(columns - 128, -128, -128)]
            new = jnp.concatenate([flip_lanes(t, 127) for t in tiles], axis=1)
            hn[i] = -new if i == 2 else new

    flux_w = packed_face(sw[...], qw[...])
    for k in range(levels):
        edge = halves[0]
        moved = pltpu.roll(flux_w, 128 - k, 1) if k else flux_w
        out_v[k, :, edge] = out_v[k, :, edge] + jnp.where(
            lanes((rows, 128)) == 0, c_v[k, :, edge] * moved, 0.0
        )
    flux_n = face(gn[0], hn[0], gn[1], hn[1], gn[2], hn[2])
    out_v[:, rows - 1, :] = out_v[:, rows - 1, :] - c_v[:, rows - 1, :] * flux_n

    for slot in range(6):
        sent(sf.at[part_low, halves[0]], UP_ST + slot)
    sent(f_v.at[:, inner, own_low, :], UP_CF)
    sent(pe, SD_E)
    sent(pw, SD_W)
    sent(gn, SD_TU)
    sent(qe, SD_TE)
    sent(qw, SD_TW)

    @pl.when(not_last | (fold_e != lon))
    def _():
        sent(pe.at[part_high], SD_EU)

    @pl.when(not_last | (fold_w != lon))
    def _():
        sent(pw.at[part_high], SD_WU)

    @pl.when(not_first)
    def _():
        for slot in range(6):
            sent(sf.at[part_low, halves[0]], DN_ST + slot)
        sent(f_v.at[:, inner, own_low, :], DN_CF)
        sent(pe.at[part_low], SD_ED)
        sent(pw.at[part_low], SD_WD)
        sent(gs, SD_TD)


def store_kernel(tr, st, o_tr, o_sf, o_zb, o_mb, sem):
    copies = [pltpu.make_async_copy(tr, o_tr, sem.at[3])]
    for f, dst in enumerate((o_sf, o_zb, o_mb)):
        copies.append(pltpu.make_async_copy(st.at[f], dst, sem.at[f]))
    for copy in copies:
        copy.start()
    for copy in copies:
        copy.wait()


def on_device(n_lat, n_lon, *args):
    levels, rows, columns = args[0].shape
    block = pltpu.VMEM((levels, rows, columns), jnp.float32)
    ext, wide = rows + 2 * HALO, columns // 128 + 1
    strip, long_strip = pltpu.VMEM((rows, 128), jnp.float32), pltpu.VMEM((ext, 128), jnp.float32)
    line = pltpu.VMEM((3, levels, columns), jnp.float32)
    tiles = (wide, ext + 2 * PAD, 128)
    scratch = [block, block, pltpu.VMEM((levels, rows, columns), jnp.int32)] + [block] * 4
    scratch += [pltpu.VMEM(tiles, jnp.float32)] * 3
    scratch += [pltpu.VMEM((n, *tiles), jnp.float32) for n in (3, 7)]
    scratch += [strip] * 2 + [long_strip] * 2 + [strip] * 4 + [line] * 4
    scratch += [
        pltpu.SemaphoreType.DMA((11,)),
        pltpu.SemaphoreType.DMA((SLOTS,)), pltpu.SemaphoreType.DMA((SLOTS,)),
        pltpu.SemaphoreType.REGULAR((11,)),
    ]
    whole = jax.ShapeDtypeStruct((levels, rows, columns), jnp.float32)
    surface = jax.ShapeDtypeStruct((rows, columns), jnp.float32)
    in_vmem = pl.BlockSpec(memory_space=pltpu.VMEM)
    anywhere = pl.BlockSpec(memory_space=pl.ANY)
    args = [pltpu.with_memory_space_constraint(a, pltpu.HBM) for a in args]
    tracer, state = pl.pallas_call(
        functools.partial(kernel, n_lat, n_lon),
        out_shape=(whole, jax.ShapeDtypeStruct((3, rows, columns), jnp.float32)),
        in_specs=[anywhere] * 8,
        out_specs=(in_vmem,) * 2,
        scratch_shapes=scratch,
        compiler_params=pltpu.CompilerParams(
            collective_id=0, has_side_effects=True, vmem_limit_bytes=32 << 20
        ),
        name="ocean",
    )(*args)
    return pl.pallas_call(
        store_kernel,
        out_shape=(whole, surface, surface, surface),
        in_specs=[in_vmem] * 2,
        out_specs=(anywhere,) * 4,
        scratch_shapes=[pltpu.SemaphoreType.DMA((4,))],
        compiler_params=pltpu.CompilerParams(vmem_limit_bytes=32 << 20),

        name="store",
    )(tracer, state)


def solution(mesh):
    whole, surface = P(None, "lat", "lon"), P("lat", "lon")
    return jax.shard_map(
        functools.partial(on_device, mesh.shape["lat"], mesh.shape["lon"]),
        mesh=mesh,
        in_specs=(whole,) * 5 + (surface,) * 3,
        out_specs=(whole, surface, surface, surface),
        check_vma=False,
    )
```

```python
import functools

import jax
import jax.numpy as jnp
from jax import lax
from jax.experimental import pallas as pl
from jax.experimental.pallas import tpu as pltpu
from jax.sharding import PartitionSpec as P

SUB = 8
HALO = 2 * SUB
RING = 8
PAD = 8
CHUNK = 8
MESH = pl.DeviceIdType.MESH

ST_N, ST_S, CF_N, CF_S = 0, 6, 12, 13
P_E, P_W, P_NE, P_SE, P_NW, P_SW = 14, 15, 16, 17, 18, 19
T_N, T_S, T_E, T_W = 20, 21, 22, 23
UP_ST, DN_ST, UP_CF, DN_CF = 0, 6, 12, 13
SD_E, SD_W, SD_EU, SD_ED, SD_WU, SD_WD = 14, 15, 16, 17, 18, 19
SD_TU, SD_TD, SD_TE, SD_TW = 20, 21, 22, 23
SLOTS = 24
N, S, E, W, NE, NW, SE, SW, FOLD, FOLD_E, FOLD_W = range(11)
OPPOSITE = (S, N, W, E, SW, SE, NW, NE, FOLD, FOLD_E, FOLD_W)


def lanes(shape):
    return lax.broadcasted_iota(jnp.int32, shape, 1)


def flip_rows(tile):
    rows = tile.shape[0]
    index = 7 - lax.broadcasted_iota(jnp.int32, (8, 128), 0)
    parts = [
        jnp.take_along_axis(tile[r : r + 8], index, axis=0) for r in range(rows - 8, -8, -8)
    ]
    return jnp.concatenate(parts, axis=0)


def flip_lanes(tile, mask):
    index = lanes((8, 128)) ^ mask
    parts = [
        jnp.take_along_axis(tile[r : r + 8], index, axis=1) for r in range(0, tile.shape[0], 8)
    ]
    return jnp.concatenate(parts, axis=0)


def kernel(
    n_lat, n_lon,
    tr, th, mk, zu, mv, sf, zb, mb,
    out_v, o_st,
    t_v, h_v, m_v, u_v, v_v, w_v, c_v,
    x_0, x_1, x_2, f_v, a_v, pe, pw, re, rw, qe, qw, se, sw, gn, gs, hn, hs,
    load_sem, send_sem, recv_sem, ready,
):
    levels, rows, columns = t_v.shape
    own_top = PAD + HALO
    top = own_top + rows
    ext = rows + 2 * HALO
    x_v = (x_0, x_1, x_2)
    lat, lon = lax.axis_index("lat"), lax.axis_index("lon")
    last, first = lat == n_lat - 1, lat == 0
    not_last, not_first = lat < n_lat - 1, lat > 0
    east, west = lax.rem(lon + 1, n_lon), lax.rem(lon + n_lon - 1, n_lon)
    mirror = n_lon - 1 - lon
    fold_e = lax.rem(2 * n_lon - 2 - lon, n_lon)
    fold_w = lax.rem(n_lon - lon, n_lon)

    low, own, high = pl.ds(PAD, HALO), pl.ds(own_top, rows), pl.ds(top, HALO)
    own_low, own_high = pl.ds(own_top, HALO), pl.ds(top - HALO, HALO)
    part_low, part_high = pl.ds(0, HALO), pl.ds(rows - HALO, HALO)
    edge_low, middle, edge_high = pl.ds(0, HALO), pl.ds(HALO, rows), pl.ds(HALO + rows, HALO)
    halves = (pl.ds(0, 128), pl.ds(128, 128))
    inner = pl.ds(0, 2)

    loads = [
        (th, h_v), (mk, m_v), (zu, u_v), (mv, v_v), (tr, t_v),
    ]
    for f, field in enumerate((sf, zb, mb)):
        for t in range(2):
            loads.append((field.at[:, halves[t]], x_v[f].at[t, own, :]))
    loads = [pltpu.make_async_copy(s, d, load_sem.at[i]) for i, (s, d) in enumerate(loads)]
    for load in loads:
        load.start()

    always = lat >= 0
    partners = {
        N: (lat + 1, lon, not_last),
        S: (lat - 1, lon, not_first),
        E: (lat, east, always),
        W: (lat, west, always),
        NE: (lat + 1, east, not_last),
        NW: (lat + 1, west, not_last),
        SE: (lat - 1, east, not_first),
        SW: (lat - 1, west, not_first),
        FOLD: (lat, mirror, last),
        FOLD_E: (lat, fold_e, last & (fold_e != lon)),
        FOLD_W: (lat, fold_w, last & (fold_w != lon)),
    }

    def order(some_lat, some_lon):
        ring = lax.rem(some_lat, RING)
        ring = jnp.where(ring < RING // 2, ring, RING + RING // 2 - 1 - ring)
        turn = lax.div(some_lat, RING)
        place = 4 * ring + 5 * turn + 13 * lax.div(some_lon, 2)
        near = 4 * (RING // 2) + 5 * ((n_lat - 1) // RING) + 13 * (n_lon // 4 - 1)
        far = (some_lat == n_lat - 1) & (some_lon >= n_lon // 2)
        swapped = some_lon + 1 - 2 * lax.rem(some_lon, 2)
        return jnp.where(far, near + 1, place) * n_lon + swapped

    mine = order(lat, lon)
    later = {p: order(*at[:2]) > mine for p, at in partners.items()}

    def is_later(p):
        return partners[p][2] & later[p]

    def is_earlier(p):
        return partners[p][2] & jnp.logical_not(later[p])

    barrier = pltpu.get_barrier_semaphore()
    for p in (W, NW, SW, FOLD, FOLD_E, FOLD_W, N, S, E, NE, SE):

        @pl.when(is_later(p))
        def _():
            pl.semaphore_signal(
                barrier, inc=1, device_id=partners[p][:2], device_id_type=MESH
            )

    def send(src, dst, out_slot, in_slot, to_lat, to_lon):
        return pltpu.make_async_remote_copy(
            src_ref=src, dst_ref=dst, send_sem=send_sem.at[out_slot],
            recv_sem=recv_sem.at[in_slot], device_id=(to_lat, to_lon), device_id_type=MESH,
        )

    def arrived(dst, in_slot):
        send(dst, dst, 0, in_slot, lat, east).wait_recv()

    def sent(src, out_slot):
        send(src, src, out_slot, 0, lat, east).wait_send()


    state = (sf, zb, mb)

    def start(p, src, dst, out_slot, in_slot):
        send(src, dst, out_slot, in_slot, *partners[p][:2]).start()

    def send_state(p):
        rows_out = part_low if p == S else part_high
        rows_in = low if p == N else high
        out_slot, in_slot = DN_ST if p == S else UP_ST, ST_S if p == N else ST_N
        for f in range(3):
            for t in range(2):
                slot = 2 * f + t
                start(
                    p, state[f].at[rows_out, halves[t]], x_v[f].at[t, rows_in, :],
                    out_slot + slot, in_slot + slot,
                )

    def send_column(p):
        rows_out = own_low if p == S else own_high
        rows_in = low if p == N else high
        start(
            p, f_v.at[:, inner, rows_out, :], f_v.at[:, inner, rows_in, :],
            DN_CF if p == S else UP_CF, CF_S if p == N else CF_N,
        )

    sides = {
        E: (pe, rw.at[middle], SD_E, P_W),
        W: (pw, re.at[middle], SD_W, P_E),
        NE: (pe.at[part_high], rw.at[edge_low], SD_EU, P_SW),
        NW: (pw.at[part_high], re.at[edge_low], SD_WU, P_SE),
        SE: (pe.at[part_low], rw.at[edge_high], SD_ED, P_NW),
        SW: (pw.at[part_low], re.at[edge_high], SD_WD, P_NE),
        FOLD_E: (pe.at[part_high], re.at[edge_high], SD_EU, P_NE),
        FOLD_W: (pw.at[part_high], rw.at[edge_high], SD_WU, P_NW),
    }
    tracers = {
        N: (gn, hs, SD_TU, T_S),
        S: (gs, hn, SD_TD, T_N),
        E: (qe, sw, SD_TE, T_W),
        W: (qw, se, SD_TW, T_E),
        FOLD: (gn, hn, SD_TU, T_N),
    }

    def send_flat(p):
        if p in sides:
            start(p, *sides[p])
        else:
            send_column(p)

    def send_to_later(group):
        for p in group:

            @pl.when(is_later(p))
            def _():
                pl.semaphore_wait(ready.at[p], 1)
                if p not in sides:
                    send_state(p)
                send_flat(p)
                if p in tracers:
                    start(p, *tracers[p])

    count = sum(jnp.where(is_earlier(p), 1, 0) for p in partners)

    def greeted():
        @pl.when(count > 0)
        def _():
            pl.semaphore_wait(barrier, count)

        for p in (E, NE, SE, FOLD, FOLD_E, FOLD_W, W, NW, SW, S, N):

            @pl.when(is_earlier(p))
            def _():
                pl.semaphore_signal(
                    ready.at[OPPOSITE[p]], inc=1, device_id=partners[p][:2],
                    device_id_type=MESH,
                )

    @pl.when(last)
    def _():
        greeted()

        @pl.when(is_earlier(FOLD))
        def _():
            send_state(FOLD)

    in_front = lax.div(mirror, 2) != 1

    for load in loads[:4]:
        load.wait()

    @pl.when(not_last)
    def _():
        greeted()

    for p in (N, S):

        @pl.when(is_earlier(p))
        def _():
            send_state(p)

    def add_level(k, sums):
        wet = m_v[k].astype(jnp.float32) * h_v[k]
        w_v[k] = wet
        return sums[0] + wet, sums[1] + wet * u_v[k], sums[2] + wet * v_v[k]

    zero = jnp.zeros((rows, columns), jnp.float32)
    depth, force_u, force_v = lax.fori_loop(0, levels, add_level, (zero, zero, zero))
    force_u, force_v = 0.05 * force_u, 0.05 * force_v
    for t in range(2):
        f_v[0, t, own, :] = depth[:, 128 * t : 128 * t + 128]
    for t in range(2):
        f_v[1, t, own, :] = force_u[:, 128 * t : 128 * t + 128]
    for t in range(2):
        f_v[2, t, own, :] = force_v[:, 128 * t : 128 * t + 128]

    @pl.when(is_earlier(FOLD) & in_front)
    def _():
        send_column(FOLD)

    for load in loads[4:]:
        load.wait()

    lane = lanes((rows, 128))
    firsts = [x_v[f][0, own, :] for f in range(3)]
    lasts = [x_v[f][1, own, :] for f in range(3)]
    for total in (depth, force_u, force_v):
        firsts.append(total[:, :128])
        lasts.append(total[:, columns - 128 :])
    pack_e = jnp.zeros((rows, 128), jnp.float32)
    pack_w = jnp.zeros((rows, 128), jnp.float32)
    for f in range(6):
        here = (lane >= HALO * f) & (lane < HALO * (f + 1))
        from_e = pltpu.roll(lasts[f], (HALO * f + HALO) % 128, 1)
        pack_e = jnp.where(here, from_e, pack_e)
        from_w = firsts[f]
        if f:
            from_w = pltpu.roll(from_w, HALO * f, 1)
        pack_w = jnp.where(here, from_w, pack_w)
    pe[...] = pack_e
    pw[...] = pack_w
    for p in (FOLD_E, FOLD_W, E, NE, SE, W, NW, SW):

        @pl.when(is_earlier(p))
        def _():
            start(p, *sides[p])

    for p in (S, N):

        @pl.when(is_earlier(p))
        def _():
            send_column(p)

    @pl.when(last & (fold_e == lon))
    def _():
        pltpu.make_async_copy(pe.at[part_high], re.at[edge_high], recv_sem.at[P_NE]).start()

    @pl.when(last & (fold_w == lon))
    def _():
        pltpu.make_async_copy(pw.at[part_high], rw.at[edge_high], recv_sem.at[P_NW]).start()


    pack_e = jnp.zeros((rows, 128), jnp.float32)
    pack_w = jnp.zeros((rows, 128), jnp.float32)
    for i, source in enumerate((t_v, w_v, u_v)):
        for k in range(levels):
            slot = i * levels + k
            pack_e = jnp.where(
                lane == slot, pltpu.roll(source[k, :, columns - 128 :], slot + 1, 1), pack_e
            )
            from_w = source[k, :, :128]
            if slot:
                from_w = pltpu.roll(from_w, slot, 1)
            pack_w = jnp.where(lane == slot, from_w, pack_w)
    qe[...] = pack_e
    qw[...] = pack_w
    for i, source in enumerate((t_v, w_v, v_v)):
        gn[i] = source[:, rows - 1, :]
        gs[i] = source[:, 0, :]
    for p in (E, FOLD, S, N, W):
        now = is_earlier(p) & in_front if p == FOLD else is_earlier(p)

        @pl.when(now)
        def _():
            start(p, *tracers[p])

    send_to_later((N, S, E, NE, SE))

    col = lanes((rows, columns))
    row = lax.broadcasted_iota(jnp.int32, (rows, columns), 0)

    def tracer_level(k, lower):
        t, w, u, v = t_v[k], w_v[k], u_v[k], v_v[k]
        t_e, w_e, u_e = (pltpu.roll(z, columns - 1, 1) for z in (t, w, u))
        flux = jnp.minimum(w, w_e) * (0.25 * (u + u_e) * (t + t_e) - 0.1 * (t_e - t))
        flux = jnp.where(col == columns - 1, 0.0, flux)
        flow = flux - pltpu.roll(flux, 1, 1)
        t_n, w_n, v_n = (pltpu.roll(z, rows - 1, 0) for z in (t, w, v))
        flux = jnp.minimum(w, w_n) * (0.25 * (v + v_n) * (t + t_n) - 0.1 * (t_n - t))
        flux = jnp.where(row == rows - 1, 0.0, flux)
        flow = flow + (flux - pltpu.roll(flux, 1, 0))
        above = jnp.minimum(k + 1, levels - 1)
        upper = 0.2 * jnp.minimum(w, w_v[above]) * (t_v[above] - t)
        scale = 0.2 * m_v[k].astype(jnp.float32) / h_v[k]
        c_v[k] = scale
        out_v[k] = t + scale * ((upper - lower) - flow)
        return upper

    lax.fori_loop(0, levels, tracer_level, zero)

    @pl.when(is_earlier(FOLD) & jnp.logical_not(in_front))
    def _():
        send_column(FOLD)
        start(FOLD, *tracers[FOLD])

    send_to_later((FOLD, FOLD_E, FOLD_W, W, NW, SW))

    def face(t_a, t_b, w_a, w_b, u_a, u_b):
        return jnp.minimum(w_a, w_b) * (0.25 * (u_a + u_b) * (t_a + t_b) - 0.1 * (t_b - t_a))

    def packed_face(a, b):
        a_1, b_1 = pltpu.roll(a, 128 - levels, 1), pltpu.roll(b, 128 - levels, 1)
        a_2, b_2 = pltpu.roll(a, 128 - 2 * levels, 1), pltpu.roll(b, 128 - 2 * levels, 1)
        return face(a, b, a_1, b_1, a_2, b_2)

    lane = lanes((rows, 128))
    arrived(se, T_E)

    @pl.when(not_first)
    def _():
        arrived(hs, T_S)

    @pl.when(first)
    def _():
        hs[...] = jnp.zeros(hs.shape, jnp.float32)

    flux_e = packed_face(qe[...], se[...])
    for k in range(levels):
        edge = halves[1]
        moved = pltpu.roll(flux_e, 127 - k, 1)
        out_v[k, :, edge] = out_v[k, :, edge] - jnp.where(
            lane == 127, c_v[k, :, edge] * moved, 0.0
        )
    flux_s = face(hs[0], gs[0], hs[1], gs[1], hs[2], gs[2])
    out_v[:, 0, :] = out_v[:, 0, :] + c_v[:, 0, :] * flux_s

    arrived(sw, T_W)
    flux_w = packed_face(sw[...], qw[...])
    for k in range(levels):
        edge = halves[0]
        moved = pltpu.roll(flux_w, 128 - k, 1) if k else flux_w
        out_v[k, :, edge] = out_v[k, :, edge] + jnp.where(
            lanes((rows, 128)) == 0, c_v[k, :, edge] * moved, 0.0
        )

    arrived(re.at[middle], P_E)
    arrived(rw.at[middle], P_W)

    @pl.when(not_first)
    def _():
        for f in range(3):
            for t in range(2):
                arrived(x_v[f].at[t, low, :], ST_S + 2 * f + t)
        arrived(f_v.at[:, inner, low, :], CF_S)
        arrived(re.at[edge_low], P_SE)
        arrived(rw.at[edge_low], P_SW)

    @pl.when(first)
    def _():
        f_v[:, inner, low, :] = jnp.zeros((3, 2, HALO, 128), jnp.float32)
        for f in range(3):
            x_v[f][inner, low, :] = jnp.zeros((2, HALO, 128), jnp.float32)
        re[edge_low] = jnp.zeros((HALO, 128), jnp.float32)
        rw[edge_low] = jnp.zeros((HALO, 128), jnp.float32)

    def join_sides(first_row, count):
        lane = lanes((count, 128))
        from_e, from_w = re[pl.ds(first_row, count)], rw[pl.ds(first_row, count)]
        for f in range(6):
            shift = (128 - HALO * f) % 128
            tile_e = pltpu.roll(from_e, shift, 1) if shift else from_e
            shift = 128 - HALO - HALO * f
            tile_w = pltpu.roll(from_w, shift, 1) if shift else from_w
            ref = x_v[f] if f < 3 else f_v.at[f - 3]
            ref[2, pl.ds(PAD + first_row, count), :] = jnp.where(lane < 64, tile_e, tile_w)

    def to_east_of(tiles):
        turned = [pltpu.roll(x, 127, 1) for x in tiles]
        edge = lanes(tiles[0].shape) == 127
        return [jnp.where(edge, turned[(t + 1) % 3], turned[t]) for t in range(3)]

    def to_west_of(tiles):
        turned = [pltpu.roll(x, 1, 1) for x in tiles]
        edge = lanes(tiles[0].shape) == 0
        return [jnp.where(edge, turned[(t + 2) % 3], turned[t]) for t in range(3)]

    def north_faces(r):
        here, north = pl.ds(r, HALO), pl.ds(r + 1, HALO)
        for t in range(3):
            a_v[3, t, here, :] = 0.5 * jnp.minimum(f_v[0, t, here, :], f_v[0, t, north, :])

    def constants(r):
        here = pl.ds(r, HALO)
        d = [f_v[0, t, here, :] for t in range(3)]
        d_e, d_w = to_east_of(d), to_west_of(d)
        for t in range(3):
            wet = jnp.minimum(2.0 * d[t], 1.0)
            a_v[0, t, here, :] = wet
            a_v[1, t, here, :] = 0.01 * wet
            a_v[2, t, here, :] = 0.5 * jnp.minimum(d[t], d_e[t])
            a_v[6, t, here, :] = 0.5 * jnp.minimum(d[t], d_w[t])
            a_v[4, t, here, :] = 0.2 * f_v[1, t, here, :]
            a_v[5, t, here, :] = 0.2 * f_v[2, t, here, :]
            x_v[0][t, here, :] = 0.05 * x_v[0][t, here, :]

    join_sides(0, HALO + rows)
    chunks = range(PAD, PAD + ext, HALO)
    for r in chunks[:-1]:
        constants(r)
    for r in chunks[:-2]:
        north_faces(r)

    for f in range(3):
        for t in range(2):
            arrived(x_v[f].at[t, high, :], ST_N + 2 * f + t)

    def flip_north(refs):
        for f, ref in enumerate(refs):
            old = [ref[t, high, :] for t in range(2)]
            for t in range(2):
                new = flip_lanes(flip_rows(old[1 - t]), 127)
                ref[t, high, :] = new if f == 0 else -new

    @pl.when(last)
    def _():
        flip_north(x_v)

    arrived(re.at[edge_high], P_NE)
    arrived(rw.at[edge_high], P_NW)
    arrived(f_v.at[:, inner, high, :], CF_N)

    @pl.when(last)
    def _():
        flip_north([f_v.at[f] for f in range(3)])
        field = lanes((HALO, 128)) // HALO
        even = (field == 0) | (field == 3)
        for ref in (re, rw):
            new = flip_lanes(flip_rows(ref[edge_high]), HALO - 1)
            ref[edge_high] = jnp.where(even, new, -new)

    join_sides(HALO + rows, HALO)
    constants(chunks[-1])
    north_faces(chunks[-2])
    north_faces(chunks[-1])

    def heights(r):
        here, north, south = pl.ds(r, CHUNK), pl.ds(r + 1, CHUNK), pl.ds(r - 1, CHUNK)
        ub = [x_1[t, here, :] for t in range(3)]
        ub_e, ub_w = to_east_of(ub), to_west_of(ub)
        for t in range(3):
            vb = x_2[t, here, :]
            out_n = a_v[3, t, here, :] * (vb + x_2[t, north, :])
            in_s = a_v[3, t, south, :] * (vb + x_2[t, south, :])
            out_e = a_v[2, t, here, :] * (ub[t] + ub_e[t])
            in_w = a_v[6, t, here, :] * (ub[t] + ub_w[t])
            div = (out_e - in_w) + (out_n - in_s)
            x_0[t, here, :] = x_0[t, here, :] - a_v[1, t, here, :] * div

    def speeds(r):
        here, north, south = pl.ds(r, CHUNK), pl.ds(r + 1, CHUNK), pl.ds(r - 1, CHUNK)
        eta = [x_0[t, here, :] for t in range(3)]
        eta_e, eta_w = to_east_of(eta), to_west_of(eta)
        for t in range(3):
            wet = a_v[0, t, here, :]
            drive = a_v[4, t, here, :] - (eta_e[t] - eta_w[t])
            x_1[t, here, :] = wet * (x_1[t, here, :] + drive)
            slope = x_0[t, north, :] - x_0[t, south, :]
            drive = a_v[5, t, here, :] - slope
            x_2[t, here, :] = wet * (x_2[t, here, :] + drive)

    def cycles(start_row, count):
        def step(_, carry):
            for r in range(start_row, start_row + count, CHUNK):
                heights(r)
                if r > start_row:
                    speeds(r - CHUNK)
            speeds(start_row + count - CHUNK)
            return carry

        lax.fori_loop(0, SUB // 2, step, 0, unroll=True)

    cycles(PAD, ext)
    cycles(PAD + SUB, ext - HALO)
    for t in range(2):
        o_st[0, :, halves[t]] = 20.0 * x_v[0][t, own, :]
        for f in range(1, 3):
            o_st[f, :, halves[t]] = x_v[f][t, own, :]

    arrived(hn, T_N)

    @pl.when(last)
    def _():
        for i in range(3):
            old = hn[i]
            tiles = [old[:, c : c + 128] for c in range(columns - 128, -128, -128)]
            new = jnp.concatenate([flip_lanes(t, 127) for t in tiles], axis=1)
            hn[i] = -new if i == 2 else new

    flux_n = face(gn[0], hn[0], gn[1], hn[1], gn[2], hn[2])
    out_v[:, rows - 1, :] = out_v[:, rows - 1, :] - c_v[:, rows - 1, :] * flux_n

    for slot in range(6):
        sent(sf.at[part_low, halves[0]], UP_ST + slot)
    sent(f_v.at[:, inner, own_low, :], UP_CF)
    sent(pe, SD_E)
    sent(pw, SD_W)
    sent(gn, SD_TU)
    sent(qe, SD_TE)
    sent(qw, SD_TW)

    @pl.when(not_last | (fold_e != lon))
    def _():
        sent(pe.at[part_high], SD_EU)

    @pl.when(not_last | (fold_w != lon))
    def _():
        sent(pw.at[part_high], SD_WU)

    @pl.when(not_first)
    def _():
        for slot in range(6):
            sent(sf.at[part_low, halves[0]], DN_ST + slot)
        sent(f_v.at[:, inner, own_low, :], DN_CF)
        sent(pe.at[part_low], SD_ED)
        sent(pw.at[part_low], SD_WD)
        sent(gs, SD_TD)


def store_kernel(tr, st, o_tr, o_sf, o_zb, o_mb, sem):
    copies = [pltpu.make_async_copy(tr, o_tr, sem.at[3])]
    for f, dst in enumerate((o_sf, o_zb, o_mb)):
        copies.append(pltpu.make_async_copy(st.at[f], dst, sem.at[f]))
    for copy in copies:
        copy.start()
    for copy in copies:
        copy.wait()


def on_device(n_lat, n_lon, *args):
    levels, rows, columns = args[0].shape
    block = pltpu.VMEM((levels, rows, columns), jnp.float32)
    ext, wide = rows + 2 * HALO, columns // 128 + 1
    strip, long_strip = pltpu.VMEM((rows, 128), jnp.float32), pltpu.VMEM((ext, 128), jnp.float32)
    line = pltpu.VMEM((3, levels, columns), jnp.float32)
    tiles = (wide, ext + 2 * PAD, 128)
    scratch = [block, block, pltpu.VMEM((levels, rows, columns), jnp.int32)] + [block] * 4
    scratch += [pltpu.VMEM(tiles, jnp.float32)] * 3
    scratch += [pltpu.VMEM((n, *tiles), jnp.float32) for n in (3, 7)]
    scratch += [strip] * 2 + [long_strip] * 2 + [strip] * 4 + [line] * 4
    scratch += [
        pltpu.SemaphoreType.DMA((11,)),
        pltpu.SemaphoreType.DMA((SLOTS,)), pltpu.SemaphoreType.DMA((SLOTS,)),
        pltpu.SemaphoreType.REGULAR((11,)),
    ]
    whole = jax.ShapeDtypeStruct((levels, rows, columns), jnp.float32)
    surface = jax.ShapeDtypeStruct((rows, columns), jnp.float32)
    in_vmem = pl.BlockSpec(memory_space=pltpu.VMEM)
    anywhere = pl.BlockSpec(memory_space=pl.ANY)
    args = [pltpu.with_memory_space_constraint(a, pltpu.HBM) for a in args]
    tracer, state = pl.pallas_call(
        functools.partial(kernel, n_lat, n_lon),
        out_shape=(whole, jax.ShapeDtypeStruct((3, rows, columns), jnp.float32)),
        in_specs=[anywhere] * 8,
        out_specs=(in_vmem,) * 2,
        scratch_shapes=scratch,
        compiler_params=pltpu.CompilerParams(
            collective_id=0, has_side_effects=True, vmem_limit_bytes=32 << 20
        ),
        name="ocean",
    )(*args)
    return pl.pallas_call(
        store_kernel,
        out_shape=(whole, surface, surface, surface),
        in_specs=[in_vmem] * 2,
        out_specs=(anywhere,) * 4,
        scratch_shapes=[pltpu.SemaphoreType.DMA((4,))],
        compiler_params=pltpu.CompilerParams(vmem_limit_bytes=32 << 20),

        name="store",
    )(tracer, state)


def solution(mesh):
    whole, surface = P(None, "lat", "lon"), P("lat", "lon")
    return jax.shard_map(
        functools.partial(on_device, mesh.shape["lat"], mesh.shape["lon"]),
        mesh=mesh,
        in_specs=(whole,) * 5 + (surface,) * 3,
        out_specs=(whole, surface, surface, surface),
        check_vma=False,
    )
```

```python
import functools

import jax
import jax.numpy as jnp
from jax import lax
from jax.experimental import pallas as pl
from jax.experimental.pallas import tpu as pltpu
from jax.sharding import PartitionSpec as P

SUB = 8
HALO = 2 * SUB
RING = 8
PAD = 8
CHUNK = 8
MESH = pl.DeviceIdType.MESH

ST_N, ST_S, CF_N, CF_S = 0, 6, 12, 13
P_E, P_W, P_NE, P_SE, P_NW, P_SW = 14, 15, 16, 17, 18, 19
T_N, T_S, T_E, T_W = 20, 21, 22, 23
UP_ST, DN_ST, UP_CF, DN_CF = 0, 6, 12, 13
SD_E, SD_W, SD_EU, SD_ED, SD_WU, SD_WD = 14, 15, 16, 17, 18, 19
SD_TU, SD_TD, SD_TE, SD_TW = 20, 21, 22, 23
SLOTS = 24
N, S, E, W, NE, NW, SE, SW, FOLD, FOLD_E, FOLD_W = range(11)
OPPOSITE = (S, N, W, E, SW, SE, NW, NE, FOLD, FOLD_E, FOLD_W)


def lanes(shape):
    return lax.broadcasted_iota(jnp.int32, shape, 1)


def flip_rows(tile):
    rows = tile.shape[0]
    index = 7 - lax.broadcasted_iota(jnp.int32, (8, 128), 0)
    parts = [
        jnp.take_along_axis(tile[r : r + 8], index, axis=0) for r in range(rows - 8, -8, -8)
    ]
    return jnp.concatenate(parts, axis=0)


def flip_lanes(tile, mask):
    index = lanes((8, 128)) ^ mask
    parts = [
        jnp.take_along_axis(tile[r : r + 8], index, axis=1) for r in range(0, tile.shape[0], 8)
    ]
    return jnp.concatenate(parts, axis=0)


def kernel(
    n_lat, n_lon,
    tr, th, mk, zu, mv, sf, zb, mb,
    out_v, o_st,
    t_v, h_v, m_v, u_v, v_v, w_v, c_v,
    x_0, x_1, x_2, f_v, a_v, pe, pw, re, rw, qe, qw, se, sw, gn, gs, hn, hs,
    load_sem, send_sem, recv_sem, ready,
):
    levels, rows, columns = t_v.shape
    own_top = PAD + HALO
    top = own_top + rows
    ext = rows + 2 * HALO
    x_v = (x_0, x_1, x_2)
    lat, lon = lax.axis_index("lat"), lax.axis_index("lon")
    last, first = lat == n_lat - 1, lat == 0
    not_last, not_first = lat < n_lat - 1, lat > 0
    east, west = lax.rem(lon + 1, n_lon), lax.rem(lon + n_lon - 1, n_lon)
    mirror = n_lon - 1 - lon
    fold_e = lax.rem(2 * n_lon - 2 - lon, n_lon)
    fold_w = lax.rem(n_lon - lon, n_lon)

    low, own, high = pl.ds(PAD, HALO), pl.ds(own_top, rows), pl.ds(top, HALO)
    own_low, own_high = pl.ds(own_top, HALO), pl.ds(top - HALO, HALO)
    part_low, part_high = pl.ds(0, HALO), pl.ds(rows - HALO, HALO)
    edge_low, middle, edge_high = pl.ds(0, HALO), pl.ds(HALO, rows), pl.ds(HALO + rows, HALO)
    halves = (pl.ds(0, 128), pl.ds(128, 128))
    inner = pl.ds(0, 2)

    loads = [
        (th, h_v), (mk, m_v), (zu, u_v), (mv, v_v), (tr, t_v),
    ]
    for f, field in enumerate((sf, zb, mb)):
        for t in range(2):
            loads.append((field.at[:, halves[t]], x_v[f].at[t, own, :]))
    loads = [pltpu.make_async_copy(s, d, load_sem.at[i]) for i, (s, d) in enumerate(loads)]
    for load in loads:
        load.start()

    always = lat >= 0
    partners = {
        N: (lat + 1, lon, not_last),
        S: (lat - 1, lon, not_first),
        E: (lat, east, always),
        W: (lat, west, always),
        NE: (lat + 1, east, not_last),
        NW: (lat + 1, west, not_last),
        SE: (lat - 1, east, not_first),
        SW: (lat - 1, west, not_first),
        FOLD: (lat, mirror, last),
        FOLD_E: (lat, fold_e, last & (fold_e != lon)),
        FOLD_W: (lat, fold_w, last & (fold_w != lon)),
    }

    def order(some_lat, some_lon):
        ring = lax.rem(some_lat, RING)
        ring = jnp.where(ring < RING // 2, ring, RING + RING // 2 - 1 - ring)
        turn = lax.div(some_lat, RING)
        place = 4 * ring + 5 * turn + 13 * lax.div(some_lon, 2)
        near = 4 * (RING // 2) + 5 * ((n_lat - 1) // RING) + 13 * (n_lon // 4 - 1)
        far = (some_lat == n_lat - 1) & (some_lon >= n_lon // 2)
        swapped = some_lon + 1 - 2 * lax.rem(some_lon, 2)
        return jnp.where(far, near + 1, place) * n_lon + swapped

    mine = order(lat, lon)
    later = {p: order(*at[:2]) > mine for p, at in partners.items()}

    def is_later(p):
        return partners[p][2] & later[p]

    def is_earlier(p):
        return partners[p][2] & jnp.logical_not(later[p])

    barrier = pltpu.get_barrier_semaphore()
    for p in (W, NW, SW, FOLD, FOLD_E, FOLD_W, N, S, E, NE, SE):

        @pl.when(is_later(p))
        def _():
            pl.semaphore_signal(
                barrier, inc=1, device_id=partners[p][:2], device_id_type=MESH
            )

    def send(src, dst, out_slot, in_slot, to_lat, to_lon):
        return pltpu.make_async_remote_copy(
            src_ref=src, dst_ref=dst, send_sem=send_sem.at[out_slot],
            recv_sem=recv_sem.at[in_slot], device_id=(to_lat, to_lon), device_id_type=MESH,
        )

    def arrived(dst, in_slot):
        send(dst, dst, 0, in_slot, lat, east).wait_recv()

    def sent(src, out_slot):
        send(src, src, out_slot, 0, lat, east).wait_send()


    state = (sf, zb, mb)

    def start(p, src, dst, out_slot, in_slot):
        send(src, dst, out_slot, in_slot, *partners[p][:2]).start()

    def send_state(p):
        rows_out = part_low if p == S else part_high
        rows_in = low if p == N else high
        out_slot, in_slot = DN_ST if p == S else UP_ST, ST_S if p == N else ST_N
        for f in range(3):
            for t in range(2):
                slot = 2 * f + t
                start(
                    p, state[f].at[rows_out, halves[t]], x_v[f].at[t, rows_in, :],
                    out_slot + slot, in_slot + slot,
                )

    def send_column(p):
        rows_out = own_low if p == S else own_high
        rows_in = low if p == N else high
        start(
            p, f_v.at[:, inner, rows_out, :], f_v.at[:, inner, rows_in, :],
            DN_CF if p == S else UP_CF, CF_S if p == N else CF_N,
        )

    sides = {
        E: (pe, rw.at[middle], SD_E, P_W),
        W: (pw, re.at[middle], SD_W, P_E),
        NE: (pe.at[part_high], rw.at[edge_low], SD_EU, P_SW),
        NW: (pw.at[part_high], re.at[edge_low], SD_WU, P_SE),
        SE: (pe.at[part_low], rw.at[edge_high], SD_ED, P_NW),
        SW: (pw.at[part_low], re.at[edge_high], SD_WD, P_NE),
        FOLD_E: (pe.at[part_high], re.at[edge_high], SD_EU, P_NE),
        FOLD_W: (pw.at[part_high], rw.at[edge_high], SD_WU, P_NW),
    }
    tracers = {
        N: (gn, hs, SD_TU, T_S),
        S: (gs, hn, SD_TD, T_N),
        E: (qe, sw, SD_TE, T_W),
        W: (qw, se, SD_TW, T_E),
        FOLD: (gn, hn, SD_TU, T_N),
    }

    def send_flat(p):
        if p in sides:
            start(p, *sides[p])
        else:
            send_column(p)

    def send_to_later(group):
        for p in group:

            @pl.when(is_later(p))
            def _():
                pl.semaphore_wait(ready.at[p], 1)
                if p not in sides:
                    send_state(p)
                send_flat(p)
                if p in tracers:
                    start(p, *tracers[p])

    count = sum(jnp.where(is_earlier(p), 1, 0) for p in partners)

    def greeted():
        @pl.when(count > 0)
        def _():
            pl.semaphore_wait(barrier, count)

    def answer():
        for p in (E, NE, SE, FOLD, FOLD_E, FOLD_W, W, NW, SW, S, N):

            @pl.when(is_earlier(p))
            def _():
                pl.semaphore_signal(
                    ready.at[OPPOSITE[p]], inc=1, device_id=partners[p][:2],
                    device_id_type=MESH,
                )

    @pl.when(last)
    def _():
        greeted()

        @pl.when(is_earlier(FOLD))
        def _():
            send_state(FOLD)

        answer()

    in_front = lax.div(mirror, 2) != 1

    for load in loads[:4]:
        load.wait()

    @pl.when(not_last)
    def _():
        greeted()
        answer()

    for p in (N, S):

        @pl.when(is_earlier(p))
        def _():
            send_state(p)

    def add_level(k, sums):
        wet = m_v[k].astype(jnp.float32) * h_v[k]
        w_v[k] = wet
        return sums[0] + wet, sums[1] + wet * u_v[k], sums[2] + wet * v_v[k]

    zero = jnp.zeros((rows, columns), jnp.float32)
    depth, force_u, force_v = lax.fori_loop(0, levels, add_level, (zero, zero, zero))
    force_u, force_v = 0.05 * force_u, 0.05 * force_v
    for t in range(2):
        f_v[0, t, own, :] = depth[:, 128 * t : 128 * t + 128]
    for t in range(2):
        f_v[1, t, own, :] = force_u[:, 128 * t : 128 * t + 128]
    for t in range(2):
        f_v[2, t, own, :] = force_v[:, 128 * t : 128 * t + 128]

    @pl.when(is_earlier(FOLD) & in_front)
    def _():
        send_column(FOLD)

    for load in loads[4:]:
        load.wait()

    lane = lanes((rows, 128))
    firsts = [x_v[f][0, own, :] for f in range(3)]
    lasts = [x_v[f][1, own, :] for f in range(3)]
    for total in (depth, force_u, force_v):
        firsts.append(total[:, :128])
        lasts.append(total[:, columns - 128 :])
    pack_e = jnp.zeros((rows, 128), jnp.float32)
    pack_w = jnp.zeros((rows, 128), jnp.float32)
    for f in range(6):
        here = (lane >= HALO * f) & (lane < HALO * (f + 1))
        from_e = pltpu.roll(lasts[f], (HALO * f + HALO) % 128, 1)
        pack_e = jnp.where(here, from_e, pack_e)
        from_w = firsts[f]
        if f:
            from_w = pltpu.roll(from_w, HALO * f, 1)
        pack_w = jnp.where(here, from_w, pack_w)
    pe[...] = pack_e
    pw[...] = pack_w
    for p in (FOLD_E, FOLD_W, E, NE, SE, W, NW, SW):

        @pl.when(is_earlier(p))
        def _():
            start(p, *sides[p])

    for p in (S, N):

        @pl.when(is_earlier(p))
        def _():
            send_column(p)

    @pl.when(last & (fold_e == lon))
    def _():
        pltpu.make_async_copy(pe.at[part_high], re.at[edge_high], recv_sem.at[P_NE]).start()

    @pl.when(last & (fold_w == lon))
    def _():
        pltpu.make_async_copy(pw.at[part_high], rw.at[edge_high], recv_sem.at[P_NW]).start()


    pack_e = jnp.zeros((rows, 128), jnp.float32)
    pack_w = jnp.zeros((rows, 128), jnp.float32)
    for i, source in enumerate((t_v, w_v, u_v)):
        for k in range(levels):
            slot = i * levels + k
            pack_e = jnp.where(
                lane == slot, pltpu.roll(source[k, :, columns - 128 :], slot + 1, 1), pack_e
            )
            from_w = source[k, :, :128]
            if slot:
                from_w = pltpu.roll(from_w, slot, 1)
            pack_w = jnp.where(lane == slot, from_w, pack_w)
    qe[...] = pack_e
    qw[...] = pack_w
    for i, source in enumerate((t_v, w_v, v_v)):
        gn[i] = source[:, rows - 1, :]
        gs[i] = source[:, 0, :]
    for p in (E, FOLD, S, N, W):
        now = is_earlier(p) & in_front if p == FOLD else is_earlier(p)

        @pl.when(now)
        def _():
            start(p, *tracers[p])

    send_to_later((N, S, E, NE, SE))

    col = lanes((rows, columns))
    row = lax.broadcasted_iota(jnp.int32, (rows, columns), 0)

    def tracer_level(k, lower):
        t, w, u, v = t_v[k], w_v[k], u_v[k], v_v[k]
        t_e, w_e, u_e = (pltpu.roll(z, columns - 1, 1) for z in (t, w, u))
        flux = jnp.minimum(w, w_e) * (0.25 * (u + u_e) * (t + t_e) - 0.1 * (t_e - t))
        flux = jnp.where(col == columns - 1, 0.0, flux)
        flow = flux - pltpu.roll(flux, 1, 1)
        t_n, w_n, v_n = (pltpu.roll(z, rows - 1, 0) for z in (t, w, v))
        flux = jnp.minimum(w, w_n) * (0.25 * (v + v_n) * (t + t_n) - 0.1 * (t_n - t))
        flux = jnp.where(row == rows - 1, 0.0, flux)
        flow = flow + (flux - pltpu.roll(flux, 1, 0))
        above = jnp.minimum(k + 1, levels - 1)
        upper = 0.2 * jnp.minimum(w, w_v[above]) * (t_v[above] - t)
        scale = 0.2 * m_v[k].astype(jnp.float32) / h_v[k]
        c_v[k] = scale
        out_v[k] = t + scale * ((upper - lower) - flow)
        return upper

    lax.fori_loop(0, levels, tracer_level, zero)

    @pl.when(is_earlier(FOLD) & jnp.logical_not(in_front))
    def _():
        send_column(FOLD)
        start(FOLD, *tracers[FOLD])

    send_to_later((FOLD, FOLD_E, FOLD_W, W, NW, SW))

    def face(t_a, t_b, w_a, w_b, u_a, u_b):
        return jnp.minimum(w_a, w_b) * (0.25 * (u_a + u_b) * (t_a + t_b) - 0.1 * (t_b - t_a))

    def packed_face(a, b):
        a_1, b_1 = pltpu.roll(a, 128 - levels, 1), pltpu.roll(b, 128 - levels, 1)
        a_2, b_2 = pltpu.roll(a, 128 - 2 * levels, 1), pltpu.roll(b, 128 - 2 * levels, 1)
        return face(a, b, a_1, b_1, a_2, b_2)

    lane = lanes((rows, 128))
    arrived(se, T_E)

    @pl.when(not_first)
    def _():
        arrived(hs, T_S)

    @pl.when(first)
    def _():
        hs[...] = jnp.zeros(hs.shape, jnp.float32)

    flux_e = packed_face(qe[...], se[...])
    for k in range(levels):
        edge = halves[1]
        moved = pltpu.roll(flux_e, 127 - k, 1)
        out_v[k, :, edge] = out_v[k, :, edge] - jnp.where(
            lane == 127, c_v[k, :, edge] * moved, 0.0
        )
    flux_s = face(hs[0], gs[0], hs[1], gs[1], hs[2], gs[2])
    out_v[:, 0, :] = out_v[:, 0, :] + c_v[:, 0, :] * flux_s

    arrived(sw, T_W)
    flux_w = packed_face(sw[...], qw[...])
    for k in range(levels):
        edge = halves[0]
        moved = pltpu.roll(flux_w, 128 - k, 1) if k else flux_w
        out_v[k, :, edge] = out_v[k, :, edge] + jnp.where(
            lanes((rows, 128)) == 0, c_v[k, :, edge] * moved, 0.0
        )

    arrived(re.at[middle], P_E)
    arrived(rw.at[middle], P_W)

    @pl.when(not_first)
    def _():
        for f in range(3):
            for t in range(2):
                arrived(x_v[f].at[t, low, :], ST_S + 2 * f + t)
        arrived(f_v.at[:, inner, low, :], CF_S)
        arrived(re.at[edge_low], P_SE)
        arrived(rw.at[edge_low], P_SW)

    @pl.when(first)
    def _():
        f_v[:, inner, low, :] = jnp.zeros((3, 2, HALO, 128), jnp.float32)
        for f in range(3):
            x_v[f][inner, low, :] = jnp.zeros((2, HALO, 128), jnp.float32)
        re[edge_low] = jnp.zeros((HALO, 128), jnp.float32)
        rw[edge_low] = jnp.zeros((HALO, 128), jnp.float32)

    def join_sides(first_row, count):
        lane = lanes((count, 128))
        from_e, from_w = re[pl.ds(first_row, count)], rw[pl.ds(first_row, count)]
        for f in range(6):
            shift = (128 - HALO * f) % 128
            tile_e = pltpu.roll(from_e, shift, 1) if shift else from_e
            shift = 128 - HALO - HALO * f
            tile_w = pltpu.roll(from_w, shift, 1) if shift else from_w
            ref = x_v[f] if f < 3 else f_v.at[f - 3]
            ref[2, pl.ds(PAD + first_row, count), :] = jnp.where(lane < 64, tile_e, tile_w)

    def to_east_of(tiles):
        turned = [pltpu.roll(x, 127, 1) for x in tiles]
        edge = lanes(tiles[0].shape) == 127
        return [jnp.where(edge, turned[(t + 1) % 3], turned[t]) for t in range(3)]

    def to_west_of(tiles):
        turned = [pltpu.roll(x, 1, 1) for x in tiles]
        edge = lanes(tiles[0].shape) == 0
        return [jnp.where(edge, turned[(t + 2) % 3], turned[t]) for t in range(3)]

    def north_faces(r):
        here, north = pl.ds(r, HALO), pl.ds(r + 1, HALO)
        for t in range(3):
            a_v[3, t, here, :] = 0.5 * jnp.minimum(f_v[0, t, here, :], f_v[0, t, north, :])

    def constants(r):
        here = pl.ds(r, HALO)
        d = [f_v[0, t, here, :] for t in range(3)]
        d_e, d_w = to_east_of(d), to_west_of(d)
        for t in range(3):
            wet = jnp.minimum(2.0 * d[t], 1.0)
            a_v[0, t, here, :] = wet
            a_v[1, t, here, :] = 0.01 * wet
            a_v[2, t, here, :] = 0.5 * jnp.minimum(d[t], d_e[t])
            a_v[6, t, here, :] = 0.5 * jnp.minimum(d[t], d_w[t])
            a_v[4, t, here, :] = 0.2 * f_v[1, t, here, :]
            a_v[5, t, here, :] = 0.2 * f_v[2, t, here, :]
            x_v[0][t, here, :] = 0.05 * x_v[0][t, here, :]

    join_sides(0, HALO + rows)
    chunks = range(PAD, PAD + ext, HALO)
    for r in chunks[:-1]:
        constants(r)
    for r in chunks[:-2]:
        north_faces(r)

    for f in range(3):
        for t in range(2):
            arrived(x_v[f].at[t, high, :], ST_N + 2 * f + t)

    def flip_north(refs):
        for f, ref in enumerate(refs):
            old = [ref[t, high, :] for t in range(2)]
            for t in range(2):
                new = flip_lanes(flip_rows(old[1 - t]), 127)
                ref[t, high, :] = new if f == 0 else -new

    @pl.when(last)
    def _():
        flip_north(x_v)

    arrived(re.at[edge_high], P_NE)
    arrived(rw.at[edge_high], P_NW)
    arrived(f_v.at[:, inner, high, :], CF_N)

    @pl.when(last)
    def _():
        flip_north([f_v.at[f] for f in range(3)])
        field = lanes((HALO, 128)) // HALO
        even = (field == 0) | (field == 3)
        for ref in (re, rw):
            new = flip_lanes(flip_rows(ref[edge_high]), HALO - 1)
            ref[edge_high] = jnp.where(even, new, -new)

    join_sides(HALO + rows, HALO)
    constants(chunks[-1])
    north_faces(chunks[-2])
    north_faces(chunks[-1])

    def heights(r):
        here, north, south = pl.ds(r, CHUNK), pl.ds(r + 1, CHUNK), pl.ds(r - 1, CHUNK)
        ub = [x_1[t, here, :] for t in range(3)]
        ub_e, ub_w = to_east_of(ub), to_west_of(ub)
        for t in range(3):
            vb = x_2[t, here, :]
            out_n = a_v[3, t, here, :] * (vb + x_2[t, north, :])
            in_s = a_v[3, t, south, :] * (vb + x_2[t, south, :])
            out_e = a_v[2, t, here, :] * (ub[t] + ub_e[t])
            in_w = a_v[6, t, here, :] * (ub[t] + ub_w[t])
            div = (out_e - in_w) + (out_n - in_s)
            x_0[t, here, :] = x_0[t, here, :] - a_v[1, t, here, :] * div

    def speeds(r):
        here, north, south = pl.ds(r, CHUNK), pl.ds(r + 1, CHUNK), pl.ds(r - 1, CHUNK)
        eta = [x_0[t, here, :] for t in range(3)]
        eta_e, eta_w = to_east_of(eta), to_west_of(eta)
        for t in range(3):
            wet = a_v[0, t, here, :]
            drive = a_v[4, t, here, :] - (eta_e[t] - eta_w[t])
            x_1[t, here, :] = wet * (x_1[t, here, :] + drive)
            slope = x_0[t, north, :] - x_0[t, south, :]
            drive = a_v[5, t, here, :] - slope
            x_2[t, here, :] = wet * (x_2[t, here, :] + drive)

    def cycles(start_row, count):
        def step(_, carry):
            for r in range(start_row, start_row + count, CHUNK):
                heights(r)
                if r > start_row:
                    speeds(r - CHUNK)
            speeds(start_row + count - CHUNK)
            return carry

        lax.fori_loop(0, SUB // 2, step, 0, unroll=True)

    cycles(PAD, ext)
    cycles(PAD + SUB, ext - HALO)
    for t in range(2):
        o_st[0, :, halves[t]] = 20.0 * x_v[0][t, own, :]
        for f in range(1, 3):
            o_st[f, :, halves[t]] = x_v[f][t, own, :]

    arrived(hn, T_N)

    @pl.when(last)
    def _():
        for i in range(3):
            old = hn[i]
            tiles = [old[:, c : c + 128] for c in range(columns - 128, -128, -128)]
            new = jnp.concatenate([flip_lanes(t, 127) for t in tiles], axis=1)
            hn[i] = -new if i == 2 else new

    flux_n = face(gn[0], hn[0], gn[1], hn[1], gn[2], hn[2])
    out_v[:, rows - 1, :] = out_v[:, rows - 1, :] - c_v[:, rows - 1, :] * flux_n

    for slot in range(6):
        sent(sf.at[part_low, halves[0]], UP_ST + slot)
    sent(f_v.at[:, inner, own_low, :], UP_CF)
    sent(pe, SD_E)
    sent(pw, SD_W)
    sent(gn, SD_TU)
    sent(qe, SD_TE)
    sent(qw, SD_TW)

    @pl.when(not_last | (fold_e != lon))
    def _():
        sent(pe.at[part_high], SD_EU)

    @pl.when(not_last | (fold_w != lon))
    def _():
        sent(pw.at[part_high], SD_WU)

    @pl.when(not_first)
    def _():
        for slot in range(6):
            sent(sf.at[part_low, halves[0]], DN_ST + slot)
        sent(f_v.at[:, inner, own_low, :], DN_CF)
        sent(pe.at[part_low], SD_ED)
        sent(pw.at[part_low], SD_WD)
        sent(gs, SD_TD)


def store_kernel(tr, st, o_tr, o_sf, o_zb, o_mb, sem):
    copies = [pltpu.make_async_copy(tr, o_tr, sem.at[3])]
    for f, dst in enumerate((o_sf, o_zb, o_mb)):
        copies.append(pltpu.make_async_copy(st.at[f], dst, sem.at[f]))
    for copy in copies:
        copy.start()
    for copy in copies:
        copy.wait()


def on_device(n_lat, n_lon, *args):
    levels, rows, columns = args[0].shape
    block = pltpu.VMEM((levels, rows, columns), jnp.float32)
    ext, wide = rows + 2 * HALO, columns // 128 + 1
    strip, long_strip = pltpu.VMEM((rows, 128), jnp.float32), pltpu.VMEM((ext, 128), jnp.float32)
    line = pltpu.VMEM((3, levels, columns), jnp.float32)
    tiles = (wide, ext + 2 * PAD, 128)
    scratch = [block, block, pltpu.VMEM((levels, rows, columns), jnp.int32)] + [block] * 4
    scratch += [pltpu.VMEM(tiles, jnp.float32)] * 3
    scratch += [pltpu.VMEM((n, *tiles), jnp.float32) for n in (3, 7)]
    scratch += [strip] * 2 + [long_strip] * 2 + [strip] * 4 + [line] * 4
    scratch += [
        pltpu.SemaphoreType.DMA((11,)),
        pltpu.SemaphoreType.DMA((SLOTS,)), pltpu.SemaphoreType.DMA((SLOTS,)),
        pltpu.SemaphoreType.REGULAR((11,)),
    ]
    whole = jax.ShapeDtypeStruct((levels, rows, columns), jnp.float32)
    surface = jax.ShapeDtypeStruct((rows, columns), jnp.float32)
    in_vmem = pl.BlockSpec(memory_space=pltpu.VMEM)
    anywhere = pl.BlockSpec(memory_space=pl.ANY)
    args = [pltpu.with_memory_space_constraint(a, pltpu.HBM) for a in args]
    tracer, state = pl.pallas_call(
        functools.partial(kernel, n_lat, n_lon),
        out_shape=(whole, jax.ShapeDtypeStruct((3, rows, columns), jnp.float32)),
        in_specs=[anywhere] * 8,
        out_specs=(in_vmem,) * 2,
        scratch_shapes=scratch,
        compiler_params=pltpu.CompilerParams(
            collective_id=0, has_side_effects=True, vmem_limit_bytes=32 << 20
        ),
        name="ocean",
    )(*args)
    return pl.pallas_call(
        store_kernel,
        out_shape=(whole, surface, surface, surface),
        in_specs=[in_vmem] * 2,
        out_specs=(anywhere,) * 4,
        scratch_shapes=[pltpu.SemaphoreType.DMA((4,))],
        compiler_params=pltpu.CompilerParams(vmem_limit_bytes=32 << 20),

        name="store",
    )(tracer, state)


def solution(mesh):
    whole, surface = P(None, "lat", "lon"), P("lat", "lon")
    return jax.shard_map(
        functools.partial(on_device, mesh.shape["lat"], mesh.shape["lon"]),
        mesh=mesh,
        in_specs=(whole,) * 5 + (surface,) * 3,
        out_specs=(whole, surface, surface, surface),
        check_vma=False,
    )
```

```python
import functools

import jax
import jax.numpy as jnp
from jax import lax
from jax.experimental import pallas as pl
from jax.experimental.pallas import tpu as pltpu
from jax.sharding import PartitionSpec as P

SUB = 8
HALO = 2 * SUB
RING = 8
PAD = 8
CHUNK = 8
MESH = pl.DeviceIdType.MESH

ST_N, ST_S, CF_N, CF_S = 0, 6, 12, 13
P_E, P_W, P_NE, P_SE, P_NW, P_SW = 14, 15, 16, 17, 18, 19
T_N, T_S, T_E, T_W = 20, 21, 22, 23
UP_ST, DN_ST, UP_CF, DN_CF = 0, 6, 12, 13
SD_E, SD_W, SD_EU, SD_ED, SD_WU, SD_WD = 14, 15, 16, 17, 18, 19
SD_TU, SD_TD, SD_TE, SD_TW = 20, 21, 22, 23
SLOTS = 24
N, S, E, W, NE, NW, SE, SW, FOLD, FOLD_E, FOLD_W = range(11)
OPPOSITE = (S, N, W, E, SW, SE, NW, NE, FOLD, FOLD_E, FOLD_W)


def lanes(shape):
    return lax.broadcasted_iota(jnp.int32, shape, 1)


def flip_rows(tile):
    rows = tile.shape[0]
    index = 7 - lax.broadcasted_iota(jnp.int32, (8, 128), 0)
    parts = [
        jnp.take_along_axis(tile[r : r + 8], index, axis=0) for r in range(rows - 8, -8, -8)
    ]
    return jnp.concatenate(parts, axis=0)


def flip_lanes(tile, mask):
    index = lanes((8, 128)) ^ mask
    parts = [
        jnp.take_along_axis(tile[r : r + 8], index, axis=1) for r in range(0, tile.shape[0], 8)
    ]
    return jnp.concatenate(parts, axis=0)


def kernel(
    n_lat, n_lon,
    tr, th, mk, zu, mv, sf, zb, mb,
    out_v, o_st,
    t_v, h_v, m_v, u_v, v_v, w_v, c_v,
    x_0, x_1, x_2, f_v, a_v, pe, pw, re, rw, qe, qw, se, sw, gn, gs, hn, hs,
    load_sem, send_sem, recv_sem, ready,
):
    levels, rows, columns = t_v.shape
    own_top = PAD + HALO
    top = own_top + rows
    ext = rows + 2 * HALO
    x_v = (x_0, x_1, x_2)
    lat, lon = lax.axis_index("lat"), lax.axis_index("lon")
    last, first = lat == n_lat - 1, lat == 0
    not_last, not_first = lat < n_lat - 1, lat > 0
    east, west = lax.rem(lon + 1, n_lon), lax.rem(lon + n_lon - 1, n_lon)
    mirror = n_lon - 1 - lon
    fold_e = lax.rem(2 * n_lon - 2 - lon, n_lon)
    fold_w = lax.rem(n_lon - lon, n_lon)

    low, own, high = pl.ds(PAD, HALO), pl.ds(own_top, rows), pl.ds(top, HALO)
    own_low, own_high = pl.ds(own_top, HALO), pl.ds(top - HALO, HALO)
    part_low, part_high = pl.ds(0, HALO), pl.ds(rows - HALO, HALO)
    edge_low, middle, edge_high = pl.ds(0, HALO), pl.ds(HALO, rows), pl.ds(HALO + rows, HALO)
    halves = (pl.ds(0, 128), pl.ds(128, 128))
    inner = pl.ds(0, 2)

    loads = [
        (th, h_v), (mk, m_v), (zu, u_v), (mv, v_v), (tr, t_v),
    ]
    for f, field in enumerate((sf, zb, mb)):
        for t in range(2):
            loads.append((field.at[:, halves[t]], x_v[f].at[t, own, :]))
    loads = [pltpu.make_async_copy(s, d, load_sem.at[i]) for i, (s, d) in enumerate(loads)]
    for load in loads:
        load.start()

    always = lat >= 0
    partners = {
        N: (lat + 1, lon, not_last),
        S: (lat - 1, lon, not_first),
        E: (lat, east, always),
        W: (lat, west, always),
        NE: (lat + 1, east, not_last),
        NW: (lat + 1, west, not_last),
        SE: (lat - 1, east, not_first),
        SW: (lat - 1, west, not_first),
        FOLD: (lat, mirror, last),
        FOLD_E: (lat, fold_e, last & (fold_e != lon)),
        FOLD_W: (lat, fold_w, last & (fold_w != lon)),
    }

    def order(some_lat, some_lon):
        ring = lax.rem(some_lat, RING)
        ring = jnp.where(ring < RING // 2, ring, RING + RING // 2 - 1 - ring)
        turn = lax.div(some_lat, RING)
        place = 4 * ring + 5 * turn + 13 * lax.div(some_lon, 2)
        near = 4 * (RING // 2) + 5 * ((n_lat - 1) // RING) + 13 * (n_lon // 4 - 1)
        far = (some_lat == n_lat - 1) & (some_lon >= n_lon // 2)
        swapped = some_lon + 1 - 2 * lax.rem(some_lon, 2)
        return jnp.where(far, near + 1, place) * n_lon + swapped

    mine = order(lat, lon)
    later = {p: order(*at[:2]) > mine for p, at in partners.items()}

    def is_later(p):
        return partners[p][2] & later[p]

    def is_earlier(p):
        return partners[p][2] & jnp.logical_not(later[p])

    barrier = pltpu.get_barrier_semaphore()
    for p in (W, NW, SW, FOLD, FOLD_E, FOLD_W, N, S, E, NE, SE):

        @pl.when(is_later(p))
        def _():
            pl.semaphore_signal(
                barrier, inc=1, device_id=partners[p][:2], device_id_type=MESH
            )

    def send(src, dst, out_slot, in_slot, to_lat, to_lon):
        return pltpu.make_async_remote_copy(
            src_ref=src, dst_ref=dst, send_sem=send_sem.at[out_slot],
            recv_sem=recv_sem.at[in_slot], device_id=(to_lat, to_lon), device_id_type=MESH,
        )

    def arrived(dst, in_slot):
        send(dst, dst, 0, in_slot, lat, east).wait_recv()

    def sent(src, out_slot):
        send(src, src, out_slot, 0, lat, east).wait_send()


    state = (sf, zb, mb)

    def start(p, src, dst, out_slot, in_slot):
        send(src, dst, out_slot, in_slot, *partners[p][:2]).start()

    def send_state(p):
        rows_out = part_low if p == S else part_high
        rows_in = low if p == N else high
        out_slot, in_slot = DN_ST if p == S else UP_ST, ST_S if p == N else ST_N
        for f in range(3):
            for t in range(2):
                slot = 2 * f + t
                start(
                    p, state[f].at[rows_out, halves[t]], x_v[f].at[t, rows_in, :],
                    out_slot + slot, in_slot + slot,
                )

    def send_column(p):
        rows_out = own_low if p == S else own_high
        rows_in = low if p == N else high
        start(
            p, f_v.at[:, inner, rows_out, :], f_v.at[:, inner, rows_in, :],
            DN_CF if p == S else UP_CF, CF_S if p == N else CF_N,
        )

    sides = {
        E: (pe, rw.at[middle], SD_E, P_W),
        W: (pw, re.at[middle], SD_W, P_E),
        NE: (pe.at[part_high], rw.at[edge_low], SD_EU, P_SW),
        NW: (pw.at[part_high], re.at[edge_low], SD_WU, P_SE),
        SE: (pe.at[part_low], rw.at[edge_high], SD_ED, P_NW),
        SW: (pw.at[part_low], re.at[edge_high], SD_WD, P_NE),
        FOLD_E: (pe.at[part_high], re.at[edge_high], SD_EU, P_NE),
        FOLD_W: (pw.at[part_high], rw.at[edge_high], SD_WU, P_NW),
    }
    tracers = {
        N: (gn, hs, SD_TU, T_S),
        S: (gs, hn, SD_TD, T_N),
        E: (qe, sw, SD_TE, T_W),
        W: (qw, se, SD_TW, T_E),
        FOLD: (gn, hn, SD_TU, T_N),
    }

    def send_flat(p):
        if p in sides:
            start(p, *sides[p])
        else:
            send_column(p)

    def send_to_later(group):
        for p in group:

            @pl.when(is_later(p))
            def _():
                pl.semaphore_wait(ready.at[p], 1)
                if p not in sides:
                    send_state(p)
                send_flat(p)
                if p in tracers:
                    start(p, *tracers[p])

    count = sum(jnp.where(is_earlier(p), 1, 0) for p in partners)

    def greeted():
        @pl.when(count > 0)
        def _():
            pl.semaphore_wait(barrier, count)

    def answer():
        for p in (E, NE, SE, FOLD, FOLD_E, FOLD_W, W, NW, SW, S, N):

            @pl.when(is_earlier(p))
            def _():
                pl.semaphore_signal(
                    ready.at[OPPOSITE[p]], inc=1, device_id=partners[p][:2],
                    device_id_type=MESH,
                )

    @pl.when(last)
    def _():
        greeted()

        @pl.when(is_earlier(FOLD))
        def _():
            send_state(FOLD)

        answer()

    in_front = lax.div(mirror, 2) != 1

    for load in loads[:4]:
        load.wait()

    @pl.when(not_last)
    def _():
        greeted()
        answer()

    for p in (N, S):

        @pl.when(is_earlier(p))
        def _():
            send_state(p)

    def add_level(k, sums):
        wet = m_v[k].astype(jnp.float32) * h_v[k]
        w_v[k] = wet
        return sums[0] + wet, sums[1] + wet * u_v[k], sums[2] + wet * v_v[k]

    zero = jnp.zeros((rows, columns), jnp.float32)
    depth, force_u, force_v = lax.fori_loop(0, levels, add_level, (zero, zero, zero))
    force_u, force_v = 0.05 * force_u, 0.05 * force_v
    for t in range(2):
        f_v[0, t, own, :] = depth[:, 128 * t : 128 * t + 128]
    for t in range(2):
        f_v[1, t, own, :] = force_u[:, 128 * t : 128 * t + 128]
    for t in range(2):
        f_v[2, t, own, :] = force_v[:, 128 * t : 128 * t + 128]

    @pl.when(is_earlier(FOLD) & in_front)
    def _():
        send_column(FOLD)

    for load in loads[4:]:
        load.wait()

    lane = lanes((rows, 128))
    firsts = [x_v[f][0, own, :] for f in range(3)]
    lasts = [x_v[f][1, own, :] for f in range(3)]
    for total in (depth, force_u, force_v):
        firsts.append(total[:, :128])
        lasts.append(total[:, columns - 128 :])
    pack_e = jnp.zeros((rows, 128), jnp.float32)
    pack_w = jnp.zeros((rows, 128), jnp.float32)
    for f in range(6):
        here = (lane >= HALO * f) & (lane < HALO * (f + 1))
        from_e = pltpu.roll(lasts[f], (HALO * f + HALO) % 128, 1)
        pack_e = jnp.where(here, from_e, pack_e)
        from_w = firsts[f]
        if f:
            from_w = pltpu.roll(from_w, HALO * f, 1)
        pack_w = jnp.where(here, from_w, pack_w)
    pe[...] = pack_e
    pw[...] = pack_w
    for p in (FOLD_E, FOLD_W, E, NE, SE, W, NW, SW):

        @pl.when(is_earlier(p))
        def _():
            start(p, *sides[p])

    for p in (S, N):

        @pl.when(is_earlier(p))
        def _():
            send_column(p)

    @pl.when(last & (fold_e == lon))
    def _():
        pltpu.make_async_copy(pe.at[part_high], re.at[edge_high], recv_sem.at[P_NE]).start()

    @pl.when(last & (fold_w == lon))
    def _():
        pltpu.make_async_copy(pw.at[part_high], rw.at[edge_high], recv_sem.at[P_NW]).start()


    pack_e = jnp.zeros((rows, 128), jnp.float32)
    pack_w = jnp.zeros((rows, 128), jnp.float32)
    for i, source in enumerate((t_v, w_v, u_v)):
        for k in range(levels):
            slot = i * levels + k
            pack_e = jnp.where(
                lane == slot, pltpu.roll(source[k, :, columns - 128 :], slot + 1, 1), pack_e
            )
            from_w = source[k, :, :128]
            if slot:
                from_w = pltpu.roll(from_w, slot, 1)
            pack_w = jnp.where(lane == slot, from_w, pack_w)
    qe[...] = pack_e
    qw[...] = pack_w
    for i, source in enumerate((t_v, w_v, v_v)):
        gn[i] = source[:, rows - 1, :]
        gs[i] = source[:, 0, :]
    for p in (E, FOLD, S, N, W):
        now = is_earlier(p) & in_front if p == FOLD else is_earlier(p)

        @pl.when(now)
        def _():
            start(p, *tracers[p])

    send_to_later((N, S, E, NE, SE))

    col = lanes((rows, columns))
    row = lax.broadcasted_iota(jnp.int32, (rows, columns), 0)

    def tracer_level(k, lower):
        t, w, u, v = t_v[k], w_v[k], u_v[k], v_v[k]
        t_e, w_e, u_e = (pltpu.roll(z, columns - 1, 1) for z in (t, w, u))
        flux = jnp.minimum(w, w_e) * (0.25 * (u + u_e) * (t + t_e) - 0.1 * (t_e - t))
        flux = jnp.where(col == columns - 1, 0.0, flux)
        flow = flux - pltpu.roll(flux, 1, 1)
        t_n, w_n, v_n = (pltpu.roll(z, rows - 1, 0) for z in (t, w, v))
        flux = jnp.minimum(w, w_n) * (0.25 * (v + v_n) * (t + t_n) - 0.1 * (t_n - t))
        flux = jnp.where(row == rows - 1, 0.0, flux)
        flow = flow + (flux - pltpu.roll(flux, 1, 0))
        above = jnp.minimum(k + 1, levels - 1)
        upper = 0.2 * jnp.minimum(w, w_v[above]) * (t_v[above] - t)
        scale = 0.2 * m_v[k].astype(jnp.float32) / h_v[k]
        c_v[k] = scale
        out_v[k] = t + scale * ((upper - lower) - flow)
        return upper

    lax.fori_loop(0, levels, tracer_level, zero)

    @pl.when(is_earlier(FOLD) & jnp.logical_not(in_front))
    def _():
        send_column(FOLD)
        start(FOLD, *tracers[FOLD])

    send_to_later((W, FOLD, FOLD_E, FOLD_W, NW, SW))

    def face(t_a, t_b, w_a, w_b, u_a, u_b):
        return jnp.minimum(w_a, w_b) * (0.25 * (u_a + u_b) * (t_a + t_b) - 0.1 * (t_b - t_a))

    def packed_face(a, b):
        a_1, b_1 = pltpu.roll(a, 128 - levels, 1), pltpu.roll(b, 128 - levels, 1)
        a_2, b_2 = pltpu.roll(a, 128 - 2 * levels, 1), pltpu.roll(b, 128 - 2 * levels, 1)
        return face(a, b, a_1, b_1, a_2, b_2)

    lane = lanes((rows, 128))
    arrived(se, T_E)

    @pl.when(not_first)
    def _():
        arrived(hs, T_S)

    @pl.when(first)
    def _():
        hs[...] = jnp.zeros(hs.shape, jnp.float32)

    flux_e = packed_face(qe[...], se[...])
    for k in range(levels):
        edge = halves[1]
        moved = pltpu.roll(flux_e, 127 - k, 1)
        out_v[k, :, edge] = out_v[k, :, edge] - jnp.where(
            lane == 127, c_v[k, :, edge] * moved, 0.0
        )
    flux_s = face(hs[0], gs[0], hs[1], gs[1], hs[2], gs[2])
    out_v[:, 0, :] = out_v[:, 0, :] + c_v[:, 0, :] * flux_s

    arrived(sw, T_W)
    flux_w = packed_face(sw[...], qw[...])
    for k in range(levels):
        edge = halves[0]
        moved = pltpu.roll(flux_w, 128 - k, 1) if k else flux_w
        out_v[k, :, edge] = out_v[k, :, edge] + jnp.where(
            lanes((rows, 128)) == 0, c_v[k, :, edge] * moved, 0.0
        )

    arrived(re.at[middle], P_E)
    arrived(rw.at[middle], P_W)

    @pl.when(not_first)
    def _():
        for f in range(3):
            for t in range(2):
                arrived(x_v[f].at[t, low, :], ST_S + 2 * f + t)
        arrived(f_v.at[:, inner, low, :], CF_S)
        arrived(re.at[edge_low], P_SE)
        arrived(rw.at[edge_low], P_SW)

    @pl.when(first)
    def _():
        f_v[:, inner, low, :] = jnp.zeros((3, 2, HALO, 128), jnp.float32)
        for f in range(3):
            x_v[f][inner, low, :] = jnp.zeros((2, HALO, 128), jnp.float32)
        re[edge_low] = jnp.zeros((HALO, 128), jnp.float32)
        rw[edge_low] = jnp.zeros((HALO, 128), jnp.float32)

    def join_sides(first_row, count):
        lane = lanes((count, 128))
        from_e, from_w = re[pl.ds(first_row, count)], rw[pl.ds(first_row, count)]
        for f in range(6):
            shift = (128 - HALO * f) % 128
            tile_e = pltpu.roll(from_e, shift, 1) if shift else from_e
            shift = 128 - HALO - HALO * f
            tile_w = pltpu.roll(from_w, shift, 1) if shift else from_w
            ref = x_v[f] if f < 3 else f_v.at[f - 3]
            ref[2, pl.ds(PAD + first_row, count), :] = jnp.where(lane < 64, tile_e, tile_w)

    def to_east_of(tiles):
        turned = [pltpu.roll(x, 127, 1) for x in tiles]
        edge = lanes(tiles[0].shape) == 127
        return [jnp.where(edge, turned[(t + 1) % 3], turned[t]) for t in range(3)]

    def to_west_of(tiles):
        turned = [pltpu.roll(x, 1, 1) for x in tiles]
        edge = lanes(tiles[0].shape) == 0
        return [jnp.where(edge, turned[(t + 2) % 3], turned[t]) for t in range(3)]

    def north_faces(r):
        here, north = pl.ds(r, HALO), pl.ds(r + 1, HALO)
        for t in range(3):
            a_v[3, t, here, :] = 0.5 * jnp.minimum(f_v[0, t, here, :], f_v[0, t, north, :])

    def constants(r):
        here = pl.ds(r, HALO)
        d = [f_v[0, t, here, :] for t in range(3)]
        d_e, d_w = to_east_of(d), to_west_of(d)
        for t in range(3):
            wet = jnp.minimum(2.0 * d[t], 1.0)
            a_v[0, t, here, :] = wet
            a_v[1, t, here, :] = 0.01 * wet
            a_v[2, t, here, :] = 0.5 * jnp.minimum(d[t], d_e[t])
            a_v[6, t, here, :] = 0.5 * jnp.minimum(d[t], d_w[t])
            a_v[4, t, here, :] = 0.2 * f_v[1, t, here, :]
            a_v[5, t, here, :] = 0.2 * f_v[2, t, here, :]
            x_v[0][t, here, :] = 0.05 * x_v[0][t, here, :]

    join_sides(0, HALO + rows)
    chunks = range(PAD, PAD + ext, HALO)
    for r in chunks[:-1]:
        constants(r)
    for r in chunks[:-2]:
        north_faces(r)

    for f in range(3):
        for t in range(2):
            arrived(x_v[f].at[t, high, :], ST_N + 2 * f + t)

    def flip_north(refs):
        for f, ref in enumerate(refs):
            old = [ref[t, high, :] for t in range(2)]
            for t in range(2):
                new = flip_lanes(flip_rows(old[1 - t]), 127)
                ref[t, high, :] = new if f == 0 else -new

    @pl.when(last)
    def _():
        flip_north(x_v)

    arrived(re.at[edge_high], P_NE)
    arrived(rw.at[edge_high], P_NW)
    arrived(f_v.at[:, inner, high, :], CF_N)

    @pl.when(last)
    def _():
        flip_north([f_v.at[f] for f in range(3)])
        field = lanes((HALO, 128)) // HALO
        even = (field == 0) | (field == 3)
        for ref in (re, rw):
            new = flip_lanes(flip_rows(ref[edge_high]), HALO - 1)
            ref[edge_high] = jnp.where(even, new, -new)

    join_sides(HALO + rows, HALO)
    constants(chunks[-1])
    north_faces(chunks[-2])
    north_faces(chunks[-1])

    def heights(r):
        here, north, south = pl.ds(r, CHUNK), pl.ds(r + 1, CHUNK), pl.ds(r - 1, CHUNK)
        ub = [x_1[t, here, :] for t in range(3)]
        ub_e, ub_w = to_east_of(ub), to_west_of(ub)
        for t in range(3):
            vb = x_2[t, here, :]
            out_n = a_v[3, t, here, :] * (vb + x_2[t, north, :])
            in_s = a_v[3, t, south, :] * (vb + x_2[t, south, :])
            out_e = a_v[2, t, here, :] * (ub[t] + ub_e[t])
            in_w = a_v[6, t, here, :] * (ub[t] + ub_w[t])
            div = (out_e - in_w) + (out_n - in_s)
            x_0[t, here, :] = x_0[t, here, :] - a_v[1, t, here, :] * div

    def speeds(r):
        here, north, south = pl.ds(r, CHUNK), pl.ds(r + 1, CHUNK), pl.ds(r - 1, CHUNK)
        eta = [x_0[t, here, :] for t in range(3)]
        eta_e, eta_w = to_east_of(eta), to_west_of(eta)
        for t in range(3):
            wet = a_v[0, t, here, :]
            drive = a_v[4, t, here, :] - (eta_e[t] - eta_w[t])
            x_1[t, here, :] = wet * (x_1[t, here, :] + drive)
            slope = x_0[t, north, :] - x_0[t, south, :]
            drive = a_v[5, t, here, :] - slope
            x_2[t, here, :] = wet * (x_2[t, here, :] + drive)

    def cycles(start_row, count):
        def step(_, carry):
            for r in range(start_row, start_row + count, CHUNK):
                heights(r)
                if r > start_row:
                    speeds(r - CHUNK)
            speeds(start_row + count - CHUNK)
            return carry

        lax.fori_loop(0, SUB // 2, step, 0, unroll=True)

    cycles(PAD, ext)
    cycles(PAD + SUB, ext - HALO)
    for t in range(2):
        o_st[0, :, halves[t]] = 20.0 * x_v[0][t, own, :]
        for f in range(1, 3):
            o_st[f, :, halves[t]] = x_v[f][t, own, :]

    arrived(hn, T_N)

    @pl.when(last)
    def _():
        for i in range(3):
            old = hn[i]
            tiles = [old[:, c : c + 128] for c in range(columns - 128, -128, -128)]
            new = jnp.concatenate([flip_lanes(t, 127) for t in tiles], axis=1)
            hn[i] = -new if i == 2 else new

    flux_n = face(gn[0], hn[0], gn[1], hn[1], gn[2], hn[2])
    out_v[:, rows - 1, :] = out_v[:, rows - 1, :] - c_v[:, rows - 1, :] * flux_n

    for slot in range(6):
        sent(sf.at[part_low, halves[0]], UP_ST + slot)
    sent(f_v.at[:, inner, own_low, :], UP_CF)
    sent(pe, SD_E)
    sent(pw, SD_W)
    sent(gn, SD_TU)
    sent(qe, SD_TE)
    sent(qw, SD_TW)

    @pl.when(not_last | (fold_e != lon))
    def _():
        sent(pe.at[part_high], SD_EU)

    @pl.when(not_last | (fold_w != lon))
    def _():
        sent(pw.at[part_high], SD_WU)

    @pl.when(not_first)
    def _():
        for slot in range(6):
            sent(sf.at[part_low, halves[0]], DN_ST + slot)
        sent(f_v.at[:, inner, own_low, :], DN_CF)
        sent(pe.at[part_low], SD_ED)
        sent(pw.at[part_low], SD_WD)
        sent(gs, SD_TD)


def store_kernel(tr, st, o_tr, o_sf, o_zb, o_mb, sem):
    copies = [pltpu.make_async_copy(tr, o_tr, sem.at[3])]
    for f, dst in enumerate((o_sf, o_zb, o_mb)):
        copies.append(pltpu.make_async_copy(st.at[f], dst, sem.at[f]))
    for copy in copies:
        copy.start()
    for copy in copies:
        copy.wait()


def on_device(n_lat, n_lon, *args):
    levels, rows, columns = args[0].shape
    block = pltpu.VMEM((levels, rows, columns), jnp.float32)
    ext, wide = rows + 2 * HALO, columns // 128 + 1
    strip, long_strip = pltpu.VMEM((rows, 128), jnp.float32), pltpu.VMEM((ext, 128), jnp.float32)
    line = pltpu.VMEM((3, levels, columns), jnp.float32)
    tiles = (wide, ext + 2 * PAD, 128)
    scratch = [block, block, pltpu.VMEM((levels, rows, columns), jnp.int32)] + [block] * 4
    scratch += [pltpu.VMEM(tiles, jnp.float32)] * 3
    scratch += [pltpu.VMEM((n, *tiles), jnp.float32) for n in (3, 7)]
    scratch += [strip] * 2 + [long_strip] * 2 + [strip] * 4 + [line] * 4
    scratch += [
        pltpu.SemaphoreType.DMA((11,)),
        pltpu.SemaphoreType.DMA((SLOTS,)), pltpu.SemaphoreType.DMA((SLOTS,)),
        pltpu.SemaphoreType.REGULAR((11,)),
    ]
    whole = jax.ShapeDtypeStruct((levels, rows, columns), jnp.float32)
    surface = jax.ShapeDtypeStruct((rows, columns), jnp.float32)
    in_vmem = pl.BlockSpec(memory_space=pltpu.VMEM)
    anywhere = pl.BlockSpec(memory_space=pl.ANY)
    args = [pltpu.with_memory_space_constraint(a, pltpu.HBM) for a in args]
    tracer, state = pl.pallas_call(
        functools.partial(kernel, n_lat, n_lon),
        out_shape=(whole, jax.ShapeDtypeStruct((3, rows, columns), jnp.float32)),
        in_specs=[anywhere] * 8,
        out_specs=(in_vmem,) * 2,
        scratch_shapes=scratch,
        compiler_params=pltpu.CompilerParams(
            collective_id=0, has_side_effects=True, vmem_limit_bytes=32 << 20
        ),
        name="ocean",
    )(*args)
    return pl.pallas_call(
        store_kernel,
        out_shape=(whole, surface, surface, surface),
        in_specs=[in_vmem] * 2,
        out_specs=(anywhere,) * 4,
        scratch_shapes=[pltpu.SemaphoreType.DMA((4,))],
        compiler_params=pltpu.CompilerParams(vmem_limit_bytes=32 << 20),

        name="store",
    )(tracer, state)


def solution(mesh):
    whole, surface = P(None, "lat", "lon"), P("lat", "lon")
    return jax.shard_map(
        functools.partial(on_device, mesh.shape["lat"], mesh.shape["lon"]),
        mesh=mesh,
        in_specs=(whole,) * 5 + (surface,) * 3,
        out_specs=(whole, surface, surface, surface),
        check_vma=False,
    )
```
